128 devices in a mesh: fluid: 4 (over y), solid: 32 (over x, z, core).
Axes of the slice: x: 4, y: 4, z: 4, core: 2. Of those that a mesh axis runs over, the one named last changes fastest.
Arguments:
- fluid_flux: bfloat16 [3, 8192, 128], P(None, ('fluid', 'solid')), may hold values from -6 to 6
- margin_blocks: bfloat16 [20480, 128, 128], P(('fluid', 'solid')), may hold values from 0 to 0.046875
- block_fluid: int32 [20480], P(('fluid', 'solid')), may hold values from 0 to 63
- block_solid: int32 [20480], P(('fluid', 'solid')), may hold values from 0 to 1023, as said below
- diag_blocks: float32 [1024, 128, 128], P('solid'), may hold values from -3 to 18, as said below
- couple_blocks: float32 [1024, 128, 128], P('solid'), may hold values from -0.15 to 0.15
- couple_offset: int32 [1024], P('solid'), may hold values from 1 to 16
Outputs:
- mapped: float32 [3, 1024, 128], P(None, 'solid')
- nodal: float32 [3, 1024, 128], P(None, 'solid')
The draws below stay inside these ranges and needn't reach their ends.
Inputs may be any that keep to these rules, and one draw needn't show every extreme that they name: `block_solid`: the solid tiles of solid index s are s * 32 to (s + 1) * 32 - 1. Among the 160 blocks of one device at most 12 have solid tiles of one solid index, and exactly 12 do for some index. block_fluid indexes the 64 fluid tiles of the device that holds the block. `diag_blocks`: each diagonal block is symmetric.
All inputs are finite; a program needn't handle non-finite values.
Results may differ from the reference program's by a relative error of at most 0.0003.
Values sent between devices are 32-bit elements; how exact they have to be, the bound alone decides.
No kernel may reach another device: no remote copies, remote signals or barrier semaphores. Data moves between devices by JAX's collectives and lax.ppermute only.
A program may use at most 64 MiB of HBM per device.

```python
import math
import jax
import jax.numpy as jnp
from jax import lax

TILE = 128
F = 3
FT_DEV = 64
B_DEV = 160
ST_DEV = 32
HALO = 16
ITERS = 3
FT = 8192
BLOCKS = 20480
ST = 1024
CAP = 12
N_FLUID = 4
N_SOLID = 32


def draw_block_solid(key, part):
    devices = N_FLUID * N_SOLID
    slots = N_SOLID * CAP

    def one_device(index):
        device_key = jax.random.fold_in(jax.random.fold_in(key, 101), index)
        key_forced, key_noise, key_order, key_tile = jax.random.split(device_key, 4)
        slot_owner = jnp.arange(slots, dtype=jnp.int32) // CAP
        home_owner = index % N_SOLID
        forced = jax.random.randint(key_forced, (), 0, N_SOLID)
        distance = jnp.abs(slot_owner - home_owner)
        distance = jnp.minimum(distance, N_SOLID - distance)
        preference = jnp.where(slot_owner == forced, 2, jnp.where(distance <= 1, 1, 0))
        noise_bits = jax.random.randint(key_noise, (slots,), 0, 2 ** 18)
        scores = (preference * 2 ** 18 + noise_bits) * slots + jnp.arange(slots, dtype=jnp.int32)
        chosen_slots = lax.top_k(scores, B_DEV)[1]
        chosen_slots = jax.random.permutation(key_order, chosen_slots)
        tile_pick = jax.random.randint(key_tile, (B_DEV,), 0, ST_DEV)
        return chosen_slots // CAP * ST_DEV + tile_pick
    return jax.vmap(one_device)(jnp.arange(devices, dtype=jnp.int32)).reshape(-1).astype(jnp.int32)


def draw_diag_blocks(key, part):
    total_tiles = ST_DEV * N_SOLID
    key_rough, key_diagonal = jax.random.split(jax.random.fold_in(key, 7))
    spread_scale = 3.0 / math.sqrt(TILE)
    base_draw = jax.random.uniform(key_diagonal, (total_tiles, TILE), jnp.float32, 0.0, 1.0)
    rough_part = jax.random.uniform(key_rough, (total_tiles, TILE, TILE), jnp.float32, -spread_scale, spread_scale)
    diagonal = 8.0 + 10.0 * base_draw ** 4
    upper_part = jnp.triu(rough_part, 1)
    symmetric = upper_part + jnp.swapaxes(upper_part, 1, 2)
    return symmetric + diagonal[:, :, None] * jnp.eye(TILE, dtype=jnp.float32)[None, :, :]


def draw_couple_blocks(key, part):
    total_tiles = ST_DEV * N_SOLID
    key_size = jax.random.fold_in(jax.random.fold_in(key, 13), 0)
    return jax.random.uniform(key_size, (total_tiles, TILE, TILE), jnp.float32, -0.15, 0.15)


def set_ends(result, own_key, smallest, top_value):
    spot = [jax.random.randint(jax.random.fold_in(own_key, axis), (), 0, length) for axis, length in enumerate(result.shape)]
    longest = result.shape.index(max(result.shape))
    neighbour = spot[:longest] + [(spot[longest] + 1) % result.shape[longest]] + spot[longest + 1:]
    return result.at[tuple(spot)].set(smallest).at[tuple(neighbour)].set(top_value)


def levels(rng, extent, cuts, smallest, high):
    level, own = 1.0, jax.random.fold_in(rng, 6)
    for position, blocks in cuts:
        heights = jnp.exp(jax.random.uniform(jax.random.fold_in(own, position), (blocks,), jnp.float32, smallest / len(cuts), high / len(cuts)))
        level = level * jnp.repeat(heights, extent[position] // blocks).reshape([-1 if axis == position else 1 for axis in range(len(extent))])
    return level


def scatter_about(key, extent, scale, bound, cuts=(), held_as=jnp.bfloat16):
    level = levels(key, extent, cuts, -0.22, 0.18) if cuts else 1.0
    values = jax.random.normal(key, extent, jnp.float32) * scale * level
    return jnp.minimum(jnp.maximum(values, -bound), bound).astype(held_as)


def setup_inputs(seed: int = 0) -> dict:
    seeds = jax.random.split(jax.random.key(seed), 8)
    return {
        "fluid_flux": scatter_about(seeds[0], (F, FT, TILE), 1.0, 6.0, ((1, 128),)),
        "margin_blocks": jnp.clip(0.046875 * jax.random.uniform(seeds[1], (BLOCKS, TILE, TILE), jnp.float32) ** levels(seeds[1], (BLOCKS, TILE, TILE), ((0, 128),), -0.2, 0.2), 0.0, 0.046875).astype(jnp.bfloat16),
        "block_fluid": set_ends(jax.random.randint(seeds[2], (BLOCKS,), 0, FT_DEV), jax.random.fold_in(seeds[2], 1), 0, FT_DEV - 1).astype(jnp.int32),
        "block_solid": draw_block_solid(jax.random.fold_in(seeds[7], 71), 0),
        "diag_blocks": draw_diag_blocks(jax.random.fold_in(seeds[7], 71), 0),
        "couple_blocks": draw_couple_blocks(jax.random.fold_in(seeds[7], 71), 0),
        "couple_offset": set_ends(jax.random.randint(seeds[6], (ST,), 1, HALO + 1), jax.random.fold_in(seeds[6], 1), 1, HALO).astype(jnp.int32),
    }


highest = lax.Precision.HIGHEST


def apply_mass(vector, diag_blocks, couple_blocks, couple_offset):
    fields = vector.shape[0]
    total_tiles = vector.shape[1]
    own_part = jnp.einsum('tij,ftj->fti', diag_blocks, vector, precision=highest)
    padded = jnp.concatenate([vector, jnp.zeros((fields, HALO, TILE), jnp.float32)], axis=1)
    picked = jnp.zeros_like(vector)
    for offset in range(1, HALO + 1):
        offset_hit = (couple_offset == offset)[None, :, None]
        picked = picked + jnp.where(offset_hit, padded[:, offset:offset + total_tiles], 0.0)
    ahead_part = jnp.einsum('tij,ftj->fti', couple_blocks, picked, precision=highest)
    back_terms = jnp.einsum('tji,ftj->fti', couple_blocks, vector, precision=highest)
    spread = jnp.zeros_like(padded)
    for offset in range(1, HALO + 1):
        offset_hit = (couple_offset == offset)[None, :, None]
        moved = jnp.where(offset_hit, back_terms, 0.0)
        spread = spread + jnp.pad(moved, ((0, 0), (offset, HALO - offset), (0, 0)))
    return own_part + ahead_part + spread[:, :total_tiles]


def field_dots(first, second):
    return jnp.sum(first * second, axis=(1, 2))


def reference(fluid_flux, margin_blocks, block_fluid, block_solid, diag_blocks, couple_blocks, couple_offset):
    total_tiles = ST_DEV * N_SOLID
    devices = N_FLUID * N_SOLID
    fields = fluid_flux.shape[0]
    flux_dev = fluid_flux.reshape(fields, devices, FT_DEV, TILE).transpose(1, 0, 2, 3)
    blocks_dev = margin_blocks.reshape(devices, B_DEV, TILE, TILE)
    fluid_ids = block_fluid.reshape(devices, B_DEV)
    solid_ids = block_solid.reshape(devices, B_DEV)

    def accumulate(running, pieces):
        flux, blocks, fluid_rows, solid_rows = pieces
        chosen = jnp.take(flux, fluid_rows, axis=1).astype(jnp.float32)
        block_terms = jnp.einsum('fbi,bij->bfj', chosen, blocks.astype(jnp.float32), precision=highest)
        return running + jax.ops.segment_sum(block_terms, solid_rows, num_segments=total_tiles), None

    start = jnp.zeros((total_tiles, fields, TILE), jnp.float32)
    outcome = lax.scan(accumulate, start, (flux_dev, blocks_dev, fluid_ids, solid_ids))
    mapped = outcome[0].transpose(1, 0, 2)

    solution = jnp.zeros_like(mapped)
    residual = mapped
    direction = mapped
    norm_now = field_dots(residual, residual)
    for iteration in range(ITERS):
        image_field = apply_mass(direction, diag_blocks, couple_blocks, couple_offset)
        step_size = norm_now / field_dots(direction, image_field)
        solution = solution + step_size[:, None, None] * direction
        residual = residual - step_size[:, None, None] * image_field
        norm_next = field_dots(residual, residual)
        direction = residual + (norm_next / norm_now)[:, None, None] * direction
        norm_now = norm_next
    return mapped, solution
```

```python
import functools

import jax
import jax.numpy as jnp
from jax import lax
from jax.experimental import pallas as pl
from jax.experimental.pallas import tpu as pltpu
from jax.sharding import PartitionSpec as P

F32 = jnp.float32
BF16 = jnp.bfloat16
LANES = 128
ROWS = 4
SHIFT = 10.5
MOMENTS = 6
VMEM = pl.BlockSpec(memory_space=pltpu.VMEM)
SMEM = pl.BlockSpec(memory_space=pltpu.SMEM)


def dot(a, b, contract=(1, 0)):
    return lax.dot_general(
        a, b, (((contract[0],), (contract[1],)), ((), ())), preferred_element_type=F32
    )


def split(x):
    high = x.astype(BF16).astype(F32)
    return high, x - high


def margin_kernel(step_blocks, owners, capacity, own_tiles, fluid_ids, solid_ids, flux, blocks, out, fields, count):
    step = pl.program_id(0)
    chunk = capacity * ROWS
    lane = lax.broadcasted_iota(jnp.int32, (1, LANES), 1)
    lane_slot = jnp.where(lane % ROWS < 3, lane // ROWS, -1)
    lane_field = lane % ROWS

    @pl.when(step == 0)
    def _():
        out[...] = jnp.zeros_like(out)
        fields[...] = jnp.zeros_like(fields)
        tiles = flux.shape[1]
        for f in range(3):
            fields[pl.ds(f, tiles, stride=ROWS), :] = flux[f].astype(F32)
        for owner in range(owners):
            count[owner] = 0
            out[pl.ds(owner * chunk + 3, 1), :] = jnp.full((1, LANES), -1.0, F32)

    for k in range(step_blocks):
        block = step * step_blocks + k
        fluid = fluid_ids[block]
        solid = solid_ids[block]
        owner = solid // own_tiles
        tile = solid - owner * own_tiles
        rank = count[owner]
        count[owner] = rank + 1
        base = owner * chunk
        picked = fields[pl.ds(pl.multiple_of(fluid * ROWS, ROWS), ROWS), :]
        term = dot(picked.astype(BF16), blocks[k])
        for f in range(3):
            out[pl.ds(base + rank * ROWS + f, 1), :] = term[f : f + 1]
        label = out[pl.ds(base + 3, 1), :]
        own_label = (tile * ROWS + lane_field).astype(F32)
        out[pl.ds(base + 3, 1), :] = jnp.where(lane_slot == rank, own_label, label)


def margin(fluid_ids, solid_ids, flux, blocks, owners, own_tiles, capacity):
    total = blocks.shape[0]
    step_blocks = 16
    return pl.pallas_call(
        functools.partial(margin_kernel, step_blocks, owners, capacity, own_tiles),
        out_shape=jax.ShapeDtypeStruct((owners * capacity * ROWS, LANES), F32),
        grid_spec=pltpu.PrefetchScalarGridSpec(
            num_scalar_prefetch=2,
            grid=(total // step_blocks,),
            in_specs=[
                pl.BlockSpec(flux.shape, lambda i, *_: (0, 0, 0)),
                pl.BlockSpec((step_blocks, LANES, LANES), lambda i, *_: (i, 0, 0)),
            ],
            out_specs=pl.BlockSpec((owners * capacity * ROWS, LANES), lambda i, *_: (0, 0)),
            scratch_shapes=[
                pltpu.VMEM((flux.shape[1] * ROWS, LANES), F32),
                pltpu.SMEM((owners,), jnp.int32),
            ],
        ),
        compiler_params=pltpu.CompilerParams(vmem_limit_bytes=16 << 20),
        name="margin",
    )(fluid_ids, solid_ids, flux, blocks)


def prepare_kernel(diag, couple, both, turned):
    row = lax.broadcasted_iota(jnp.int32, (LANES, LANES), 0)
    column = lax.broadcasted_iota(jnp.int32, (LANES, LANES), 1)
    shift = jnp.where(row == column, SHIFT, 0.0).astype(F32)
    for t in range(diag.shape[0]):
        high, low = split(diag[t] - shift)
        both[t, 0:LANES, 0:LANES] = high.astype(BF16)
        both[t, LANES : 2 * LANES, 0:LANES] = low.astype(BF16)
        high, low = split(couple[t])
        both[t, 0:LANES, LANES : 2 * LANES] = high.astype(BF16)
        both[t, LANES : 2 * LANES, LANES : 2 * LANES] = low.astype(BF16)
        turned[t, 0:LANES, :] = high.T.astype(BF16)
        turned[t, LANES : 2 * LANES, :] = low.T.astype(BF16)


def prepare(diag, couple):
    tiles = diag.shape[0]
    step = 8
    return pl.pallas_call(
        prepare_kernel,
        out_shape=(
            jax.ShapeDtypeStruct((tiles, 2 * LANES, 2 * LANES), BF16),
            jax.ShapeDtypeStruct((tiles, 2 * LANES, LANES), BF16),
        ),
        grid=(tiles // step,),
        in_specs=[pl.BlockSpec((step, LANES, LANES), lambda i: (i, 0, 0))] * 2,
        out_specs=(
            pl.BlockSpec((step, 2 * LANES, 2 * LANES), lambda i: (i, 0, 0)),
            pl.BlockSpec((step, 2 * LANES, LANES), lambda i: (i, 0, 0)),
        ),
        compiler_params=pltpu.CompilerParams(vmem_limit_bytes=16 << 20),
        cost_estimate=pl.CostEstimate(flops=1 << 26, bytes_accessed=10 << 20, transcendentals=0),
        name="prepare",
    )(diag, couple)


def combine_kernel(owners, received, out):
    chunk = received.shape[0] // owners
    row = lax.broadcasted_iota(jnp.int32, (out.shape[0], chunk), 0).astype(F32)
    total = jnp.zeros(out.shape, F32)
    for source in range(owners):
        values = received[source * chunk : (source + 1) * chunk, :]
        label = received[source * chunk + 3 : source * chunk + 4, 0:chunk]
        hits = (row == label).astype(F32).astype(BF16)
        high, low = split(values)
        total = total + dot(hits, high.astype(BF16)) + dot(hits, low.astype(BF16))
    out[...] = total


def combine(received, owners, own_tiles):
    return pl.pallas_call(
        functools.partial(combine_kernel, owners),
        out_shape=jax.ShapeDtypeStruct((own_tiles * ROWS, LANES), F32),
        in_specs=[VMEM],
        out_specs=VMEM,
        compiler_params=pltpu.CompilerParams(vmem_limit_bytes=16 << 20),
        name="combine",
    )(received)


def put_pairs(pairs, t, value):
    high, low = split(value)
    pairs[t, 0:ROWS, :] = high
    pairs[t, ROWS : 2 * ROWS, :] = low


def load_pairs(pairs, t):
    both = pairs[t].astype(BF16)
    return jnp.concatenate([both, both], axis=1)


def fold(product):
    return product[0:ROWS] + product[ROWS : 2 * ROWS]


def local_part(tiles, offsets, pairs, spread, both, turned):
    spread[...] = jnp.zeros_like(spread)
    for t in range(tiles):
        partner = t + offsets[t]
        ahead = fold(dot(load_pairs(pairs, partner), turned[t]))
        here = fold(dot(load_pairs(pairs, t), both[t]))
        spread[t] = spread[t] + here[:, 0:LANES] + ahead
        spread[partner] = spread[partner] + here[:, LANES : 2 * LANES]


def select(flag, first, second):
    return jnp.where(flag > 0, first, second)


def first_kernel(tiles, halo, offsets, odd, part0, part1, part2, part3, both, turned, mapped, vector, image, near, far, pairs, spread):
    total = (part0[...] + part1[...]) + (part2[...] + part3[...])
    vector[...] = total
    for f in range(3):
        mapped[f] = vector[pl.ds(f, tiles, stride=ROWS), :]
    for t in range(tiles):
        put_pairs(pairs, t, vector[t * ROWS : (t + 1) * ROWS, :])
    for t in range(tiles, tiles + halo):
        pairs[t] = jnp.zeros((2 * ROWS, LANES), F32)
    local_part(tiles, offsets, pairs, spread, both, turned)
    for t in range(tiles):
        image[t * ROWS : (t + 1) * ROWS, :] = spread[t]
    flag = odd[0]
    for t in range(halo):
        rim = vector[t * ROWS : (t + 1) * ROWS, :]
        out = spread[tiles + t]
        near[t * ROWS : (t + 1) * ROWS, :] = select(flag, rim, out)
        far[t * ROWS : (t + 1) * ROWS, :] = select(flag, out, rim)


def finish_part(tiles, halo, offsets, flag, image, near, far, pairs, turned):
    for t in range(halo):
        rows = slice(t * ROWS, (t + 1) * ROWS)
        put_pairs(pairs, tiles + t, select(flag, far[rows, :], near[rows, :]))
    for t in range(tiles - halo, tiles):
        pairs[t] = jnp.zeros((2 * ROWS, LANES), F32)
    values = []
    for t in range(tiles):
        rows = slice(t * ROWS, (t + 1) * ROWS)
        value = image[rows, :]
        if t < halo:
            value = value + select(flag, near[rows, :], far[rows, :])
        if t >= tiles - halo:
            partner = jnp.maximum(t + offsets[t], tiles - halo)
            value = value + fold(dot(load_pairs(pairs, partner), turned[t]))
        values.append(value)
    return values


def second_kernel(tiles, halo, offsets, odd, image, near, far, both, turned, vector, image2, leaving, near2, far2, pairs, spread):
    flag = odd[0]
    values = finish_part(tiles, halo, offsets, flag, image, near, far, pairs, turned)
    for t in range(tiles):
        vector[t * ROWS : (t + 1) * ROWS, :] = values[t]
    for t in range(tiles):
        put_pairs(pairs, t, vector[t * ROWS : (t + 1) * ROWS, :])
    for t in range(tiles, tiles + halo):
        pairs[t] = jnp.zeros((2 * ROWS, LANES), F32)
    local_part(tiles, offsets, pairs, spread, both, turned)
    size = halo * ROWS
    for t in range(tiles):
        image2[t * ROWS : (t + 1) * ROWS, :] = spread[t]
    for t in range(halo):
        leaving[t * ROWS : (t + 1) * ROWS, :] = spread[tiles + t]
    near2[0:size, :] = select(flag, vector[0:size, :], leaving[...])
    far2[0:size, :] = select(flag, leaving[...], vector[0:size, :])
    near2[size : 2 * size, :] = image2[0:size, :]
    far2[size : 2 * size, :] = image2[0:size, :]


def third_kernel(tiles, halo, offsets, odd, last, start, vector1, image, leaving, near, far, both, turned, vector2, out, pairs, product):
    flag = odd[0]
    size = halo * ROWS
    values = finish_part(tiles, halo, offsets, flag, image, near, far, pairs, turned)
    for t in range(tiles):
        vector2[t * ROWS : (t + 1) * ROWS, :] = values[t]
    for t in range(tiles):
        put_pairs(pairs, t, vector2[t * ROWS : (t + 1) * ROWS, :])
    inside = jnp.where(last[0] > 0, 0.0, 1.0).astype(F32)
    for t in range(halo):
        rows = slice(t * ROWS, (t + 1) * ROWS)
        other = slice(size + t * ROWS, size + (t + 1) * ROWS)
        rim = select(flag, far[other, :], near[other, :]) + leaving[rows, :]
        put_pairs(pairs, tiles + t, rim * inside)
    for t in range(tiles):
        ahead = fold(dot(load_pairs(pairs, t + offsets[t]), turned[t]))
        here = fold(dot(load_pairs(pairs, t), both[t, :, 0:LANES]))
        product[t * ROWS : (t + 1) * ROWS, :] = here + 2.0 * ahead
    v0, v1, v2, v3 = start[...], vector1[...], vector2[...], product[...]
    field = lax.broadcasted_iota(jnp.int32, (2 * ROWS, LANES), 0)
    lane = lax.broadcasted_iota(jnp.int32, (2 * ROWS, LANES), 1)
    row = jnp.zeros((2 * ROWS, LANES), F32)
    for k, (a, b) in enumerate(((v0, v0), (v0, v1), (v1, v1), (v1, v2), (v2, v2), (v2, v3))):
        folded = jnp.sum((a * b).reshape(tiles * ROWS // (2 * ROWS), 2 * ROWS, LANES), axis=0)
        moment = jnp.sum(folded, axis=1, keepdims=True)
        row = row + jnp.where(lane == k * ROWS + field % ROWS, moment, 0.0)
    row = jnp.sum(row, axis=0, keepdims=True)
    out[...] = jnp.broadcast_to(row[:, None, :], out.shape)


def last_kernel(tiles, moments, start, vector1, vector2, nodal, mixed):
    total = jnp.sum(moments[...], axis=0)
    total = jnp.broadcast_to(total, (2 * ROWS, LANES))
    g = [total if k == 0 else pltpu.roll(total, LANES - k * ROWS, 1) for k in range(MOMENTS)]
    h = [g[k + 1] + SHIFT * g[k] for k in range(MOMENTS - 1)]

    def form(table, c):
        n = len(c)
        result = None
        for i in range(n):
            for j in range(i, n):
                term = (c[i] * c[j]) * table[i + j]
                term = term if i == j else 2.0 * term
                result = term if result is None else result + term
        return result

    def apply(c):
        n = len(c)
        shifted = [SHIFT * c[0]]
        for i in range(1, n):
            shifted.append(c[i - 1] + SHIFT * c[i])
        return shifted + [c[n - 1]]

    one = jnp.ones_like(total)
    rr = g[0]
    alpha = rr / h[0]
    coefficients = [alpha]
    residual = [one - alpha * SHIFT, -alpha]
    new = form(g, residual)
    beta = new / rr
    direction = [residual[0] + beta, residual[1]]
    rr = new
    alpha = rr / form(h, direction)
    coefficients = [coefficients[0] + alpha * direction[0], alpha * direction[1]]
    image = apply(direction)
    residual = [residual[0] - alpha * image[0], residual[1] - alpha * image[1], -alpha * image[2]]
    new = form(g, residual)
    beta = new / rr
    direction = [residual[0] + beta * direction[0], residual[1] + beta * direction[1], residual[2]]
    rr = new
    alpha = rr / form(h, direction)
    coefficients = [
        coefficients[0] + alpha * direction[0],
        coefficients[1] + alpha * direction[1],
        alpha * direction[2],
    ]
    field = lax.broadcasted_iota(jnp.int32, (2 * ROWS, LANES), 0)
    lane = lax.broadcasted_iota(jnp.int32, (2 * ROWS, LANES), 1)
    result = jnp.zeros(start.shape, F32).reshape(-1, 2 * ROWS, LANES)
    for c, v in zip(coefficients, (start, vector1, vector2)):
        column = jnp.sum(jnp.where(lane == field % ROWS, c, 0.0), axis=1, keepdims=True)
        result = result + column[None] * v[...].reshape(-1, 2 * ROWS, LANES)
    mixed[...] = result.reshape(start.shape)
    for f in range(3):
        nodal[f] = mixed[pl.ds(f, tiles, stride=ROWS), :]


def call(kernel, shapes, smem, vmem, scratch, name, limit=32):
    return pl.pallas_call(
        kernel,
        out_shape=tuple(jax.ShapeDtypeStruct(s, F32) for s in shapes),
        in_specs=[SMEM] * len(smem) + [VMEM] * len(vmem),
        out_specs=tuple(VMEM for _ in shapes),
        scratch_shapes=scratch,
        compiler_params=pltpu.CompilerParams(vmem_limit_bytes=limit << 20),
        name=name,
    )(*smem, *vmem)


def exchange(near, far, axis):
    n = lax.axis_size(axis)
    far_route = [(i, i + 1) for i in range(1, n - 1, 2)] + [(i + 1, i) for i in range(1, n - 1, 2)]
    near_route = [(i, i ^ 1) for i in range(n)]
    return lax.ppermute(near, axis, near_route), lax.ppermute(far, axis, far_route)


def local(fluid_flux, margin_blocks, block_fluid, block_solid, diag_blocks, couple_blocks, couple_offset):
    owners = lax.axis_size("solid")
    groups = lax.axis_size("fluid")
    tiles = diag_blocks.shape[0]
    halo = tiles // 2
    total_blocks = block_fluid.shape[0]
    capacity = 5 * total_blocks // (2 * owners)
    place = lax.axis_index("solid")
    odd = (place % 2).astype(jnp.int32).reshape(1)
    last = (place == owners - 1).astype(jnp.int32).reshape(1)

    sent = margin(block_fluid, block_solid, fluid_flux, margin_blocks, owners, tiles, capacity)
    received = lax.all_to_all(sent, "solid", split_axis=0, concat_axis=0, tiled=True)
    both, turned = prepare(diag_blocks, couple_blocks)
    part = combine(received, owners, tiles)
    parts = [part] + [
        lax.ppermute(part, "fluid", [(i, i ^ d) for i in range(groups)]) for d in (1, 2, 3)
    ]
    whole = (tiles * ROWS, LANES)
    half = (halo * ROWS, LANES)
    pairs = pltpu.VMEM((tiles + halo, 2 * ROWS, LANES), F32)
    spread = pltpu.VMEM((tiles + halo, ROWS, LANES), F32)
    (mapped, start, image, near, far) = call(
        functools.partial(first_kernel, tiles, halo),
        ((3, tiles, LANES), whole, whole, half, half),
        (couple_offset, odd),
        (*parts, both, turned),
        [pairs, spread],
        "first",
    )
    near, far = exchange(near, far, "solid")
    (vector1, image, leaving, near, far) = call(
        functools.partial(second_kernel, tiles, halo),
        (whole, whole, half, whole, whole),
        (couple_offset, odd),
        (image, near, far, both, turned),
        [pairs, spread],
        "second",
    )
    near, far = exchange(near, far, "solid")
    vector2, moments = call(
        functools.partial(third_kernel, tiles, halo),
        (whole, (owners, 1, LANES)),
        (couple_offset, odd, last),
        (start, vector1, image, leaving, near, far, both, turned),
        [pairs, pltpu.VMEM(whole, F32)],
        "third",
    )
    moments = lax.all_to_all(moments, "solid", split_axis=0, concat_axis=0, tiled=True)
    (nodal,) = call(
        functools.partial(last_kernel, tiles),
        ((3, tiles, LANES),),
        (),
        (moments, start, vector1, vector2),
        [pltpu.VMEM(whole, F32)],
        "last",
    )
    return mapped, nodal


def solution(mesh):
    in_specs = (
        P(None, ("fluid", "solid"), None),
        P(("fluid", "solid"), None, None),
        P(("fluid", "solid")),
        P(("fluid", "solid")),
        P("solid", None, None),
        P("solid", None, None),
        P("solid"),
    )
    out_specs = (P(None, "solid", None), P(None, "solid", None))
    return jax.shard_map(local, mesh=mesh, in_specs=in_specs, out_specs=out_specs, check_vma=False)
```

```python
import functools

import jax
import jax.numpy as jnp
from jax import lax
from jax.experimental import pallas as pl
from jax.experimental.pallas import tpu as pltpu
from jax.sharding import PartitionSpec as P

F32 = jnp.float32
BF16 = jnp.bfloat16
LANES = 128
ROWS = 4
SHIFT = 10.5
MOMENTS = 6
VMEM = pl.BlockSpec(memory_space=pltpu.VMEM)
SMEM = pl.BlockSpec(memory_space=pltpu.SMEM)
HBM = pl.BlockSpec(memory_space=pltpu.HBM)


def in_hbm(x):
    return pltpu.with_memory_space_constraint(x, pltpu.HBM)


def dot(a, b, contract=(1, 0)):
    return lax.dot_general(
        a, b, (((contract[0],), (contract[1],)), ((), ())), preferred_element_type=F32
    )


def split(x):
    high = x.astype(BF16).astype(F32)
    return high, x - high


def margin_kernel(owners, own_tiles, chunk, fluid_hbm, solid_hbm, flux_hbm, blocks_hbm, out, blocks, flux, fields, fluid_ids, solid_ids, count, sems):
    pieces = sems.shape[0] - 3
    size = blocks.shape[0] // pieces
    small = [
        pltpu.make_async_copy(source, target, sems.at[pieces + k])
        for k, (source, target) in enumerate(
            ((fluid_hbm, fluid_ids), (solid_hbm, solid_ids), (flux_hbm, flux))
        )
    ]

    def piece(k):
        rows = pl.ds(k * size, size)
        return pltpu.make_async_copy(blocks_hbm.at[rows], blocks.at[rows], sems.at[k])

    for copy in small:
        copy.start()
    for k in range(pieces):
        piece(k).start()
    label_row = chunk - ROWS
    lane = lax.broadcasted_iota(jnp.int32, (1, LANES), 1)
    lane_slot = jnp.where(lane < label_row, lane // 3, -1)
    lane_field = lane % 3
    out[...] = jnp.zeros_like(out)
    fields[...] = jnp.zeros_like(fields)
    for owner in range(owners):
        count[owner] = 0
        out[pl.ds(owner * chunk + label_row, 1), :] = jnp.full((1, LANES), -1.0, F32)
    for copy in small:
        copy.wait()
    for f in range(3):
        fields[pl.ds(f, flux.shape[1], stride=ROWS), :] = flux[f].astype(F32)

    def one_piece(k, _):
        piece(k).wait()
        for j in range(size):
            block = k * size + j
            fluid = fluid_ids[block]
            solid = solid_ids[block]
            owner = solid // own_tiles
            tile = solid - owner * own_tiles
            rank = count[owner]
            count[owner] = rank + 1
            base = owner * chunk
            picked = fields[pl.ds(pl.multiple_of(fluid * ROWS, ROWS), ROWS), :]
            term = dot(picked.astype(BF16), blocks[block])
            for f in range(3):
                out[pl.ds(base + rank * 3 + f, 1), :] = term[f : f + 1]
            label = out[pl.ds(base + label_row, 1), :]
            own_label = (tile * ROWS + lane_field).astype(F32)
            out[pl.ds(base + label_row, 1), :] = jnp.where(lane_slot == rank, own_label, label)
        return 0

    lax.fori_loop(0, pieces, one_piece, 0)


def margin(fluid_ids, solid_ids, flux, blocks, owners, own_tiles, chunk):
    pieces = 10
    return pl.pallas_call(
        functools.partial(margin_kernel, owners, own_tiles, chunk),
        out_shape=jax.ShapeDtypeStruct((owners * chunk, LANES), F32),
        in_specs=[HBM] * 4,
        out_specs=VMEM,
        scratch_shapes=[
            pltpu.VMEM(blocks.shape, BF16),
            pltpu.VMEM(flux.shape, BF16),
            pltpu.VMEM((flux.shape[1] * ROWS, LANES), F32),
            pltpu.SMEM(fluid_ids.shape, jnp.int32),
            pltpu.SMEM(solid_ids.shape, jnp.int32),
            pltpu.SMEM((owners,), jnp.int32),
            pltpu.SemaphoreType.DMA((pieces + 3,)),
        ],
        compiler_params=pltpu.CompilerParams(vmem_limit_bytes=12 << 20),
        name="margin",
    )(*(in_hbm(x) for x in (fluid_ids, solid_ids, flux, blocks)))


def prepare_kernel(diag_hbm, couple_hbm, matrices, diag, couple, sems):
    pieces = sems.shape[1]
    size = diag.shape[0] // pieces

    def piece(k):
        part = pl.ds(k * size, size)
        return [
            pltpu.make_async_copy(source.at[part], target.at[part], sems.at[i, k])
            for i, (source, target) in enumerate(((diag_hbm, diag), (couple_hbm, couple)))
        ]

    for k in range(pieces):
        for copy in piece(k):
            copy.start()
    row = lax.broadcasted_iota(jnp.int32, (LANES, LANES), 0)
    column = lax.broadcasted_iota(jnp.int32, (LANES, LANES), 1)
    shift = jnp.where(row == column, SHIFT, 0.0).astype(F32)
    for k in range(pieces):
        for copy in piece(k):
            copy.wait()
        for t in range(k * size, (k + 1) * size):
            high, low = split(diag[t] - shift)
            matrices[t, 0:LANES, :] = high.astype(BF16)
            matrices[t, LANES : 2 * LANES, :] = low.astype(BF16)
            high, low = split(couple[t])
            matrices[t, 2 * LANES : 3 * LANES, :] = high.astype(BF16)
            matrices[t, 3 * LANES : 4 * LANES, :] = low.astype(BF16)
            matrices[t, 4 * LANES : 5 * LANES, :] = high.T.astype(BF16)
            matrices[t, 5 * LANES : 6 * LANES, :] = low.T.astype(BF16)


def prepare(diag, couple):
    tiles = diag.shape[0]
    return pl.pallas_call(
        prepare_kernel,
        out_shape=jax.ShapeDtypeStruct((tiles, 6 * LANES, LANES), BF16),
        in_specs=[HBM] * 2,
        out_specs=VMEM,
        scratch_shapes=[
            pltpu.VMEM(diag.shape, F32),
            pltpu.VMEM(couple.shape, F32),
            pltpu.SemaphoreType.DMA((2, 4)),
        ],
        compiler_params=pltpu.CompilerParams(vmem_limit_bytes=12 << 20),
        cost_estimate=pl.CostEstimate(flops=1 << 26, bytes_accessed=10 << 20, transcendentals=0),
        name="prepare",
    )(in_hbm(diag), in_hbm(couple))


def views(matrices):
    return tuple(matrices.at[:, 2 * k * LANES : 2 * (k + 1) * LANES, :] for k in range(3))


def combine_kernel(owners, received, out):
    chunk = received.shape[0] // owners
    row = lax.broadcasted_iota(jnp.int32, (out.shape[0], chunk), 0).astype(F32)
    total = jnp.zeros(out.shape, F32)
    for source in range(owners):
        values = received[source * chunk : (source + 1) * chunk, :]
        label = received[(source + 1) * chunk - ROWS : (source + 1) * chunk - ROWS + 1, 0:chunk]
        hits = (row == label).astype(F32).astype(BF16)
        high, low = split(values)
        total = total + dot(hits, high.astype(BF16)) + dot(hits, low.astype(BF16))
    out[...] = total


def combine(received, owners, own_tiles):
    return pl.pallas_call(
        functools.partial(combine_kernel, owners),
        out_shape=jax.ShapeDtypeStruct((own_tiles * ROWS, LANES), F32),
        in_specs=[VMEM],
        out_specs=VMEM,
        compiler_params=pltpu.CompilerParams(vmem_limit_bytes=16 << 20),
        name="combine",
    )(received)


def put_pairs(pairs, t, value):
    high, low = split(value)
    pairs[t, 0:ROWS, :] = high
    pairs[t, ROWS : 2 * ROWS, :] = low


def load_pairs(pairs, t):
    both = pairs[t].astype(BF16)
    return jnp.concatenate([both, both], axis=1)


def fold(product):
    return product[0:ROWS] + product[ROWS : 2 * ROWS]


def ahead(t, partner, pairs, turned):
    return fold(dot(load_pairs(pairs, partner), turned[t]))


def here(t, pairs, matrix):
    return fold(dot(load_pairs(pairs, t), matrix[t]))


def rows(t, count=1):
    return slice(t * ROWS, (t + count) * ROWS)


def select(flag, first, second):
    return jnp.where(flag > 0, first, second)


def leave(tiles, halo, offsets, pairs, spread, back, first):
    for t in range(first, tiles):
        partner = t + offsets[t]
        spread[partner] = spread[partner] + here(t, pairs, back)


def first_send_kernel(tiles, halo, offsets, place, part0, part1, part2, part3, matrices, vector, kept, near, far, pairs, spread):
    own, back, turned = views(matrices)
    vector[...] = (part0[...] + part1[...]) + (part2[...] + part3[...])
    for t in range(halo, tiles):
        put_pairs(pairs, t, vector[rows(t), :])
    spread[...] = jnp.zeros_like(spread)
    leave(tiles, halo, offsets, pairs, spread, back, halo)
    flag = place[0] % 2
    for t in range(halo):
        rim = vector[rows(t), :]
        out = spread[tiles + t]
        near[rows(t), :] = select(flag, rim, out)
        far[rows(t), :] = select(flag, out, rim)
        kept[rows(t), :] = spread[halo + t]


def first_rest_kernel(tiles, halo, offsets, vector, kept, matrices, mapped, image, pairs, spread):
    own, back, turned = views(matrices)
    for f in range(3):
        mapped[f] = vector[pl.ds(f, tiles, stride=ROWS), :]
    for t in range(tiles):
        put_pairs(pairs, t, vector[rows(t), :])
    for t in range(tiles, tiles + halo):
        pairs[t] = jnp.zeros((2 * ROWS, LANES), F32)
    for t in range(halo):
        spread[t] = jnp.zeros((ROWS, LANES), F32)
        spread[halo + t] = kept[rows(t), :]
    for t in range(tiles):
        partner = t + offsets[t]
        spread[t] = spread[t] + (here(t, pairs, own) + ahead(t, partner, pairs, turned))
        if t < halo:
            spread[partner] = spread[partner] + here(t, pairs, back)
    for t in range(tiles):
        image[rows(t), :] = spread[t]


def put_rim(tiles, halo, flag, near, far, pairs):
    for t in range(halo):
        put_pairs(pairs, tiles + t, select(flag, far[rows(t), :], near[rows(t), :]))
        pairs[tiles - halo + t] = jnp.zeros((2 * ROWS, LANES), F32)


def second_send_kernel(tiles, halo, offsets, place, image, far, near, matrices, vector, inner, kept, leaving, near2, far2, pairs, spread):
    own, back, turned = views(matrices)
    flag = place[0] % 2
    put_rim(tiles, halo, flag, near, far, pairs)
    for t in range(halo):
        vector[rows(t), :] = image[rows(t), :] + select(flag, near[rows(t), :], far[rows(t), :])
    for t in range(halo, tiles):
        partner = jnp.maximum(t + offsets[t], halo)
        vector[rows(t), :] = image[rows(t), :] + ahead(t, partner, pairs, turned)
    for t in range(tiles):
        put_pairs(pairs, t, vector[rows(t), :])
    spread[...] = jnp.zeros_like(spread)
    leave(tiles, halo, offsets, pairs, spread, back, 0)
    size = halo * ROWS
    for t in range(halo):
        inner[rows(t), :] = spread[t] + (here(t, pairs, own) + ahead(t, t + offsets[t], pairs, turned))
        kept[rows(t), :] = spread[halo + t]
        leaving[rows(t), :] = spread[tiles + t]
    near2[0:size, :] = select(flag, vector[0:size, :], leaving[...])
    far2[0:size, :] = select(flag, leaving[...], vector[0:size, :])
    near2[size : 2 * size, :] = inner[...]
    far2[size : 2 * size, :] = inner[...]


def moment(a, b):
    folded = jnp.sum((a * b).reshape(-1, 2 * ROWS, LANES), axis=0)
    return jnp.sum(folded, axis=1, keepdims=True)


def placed(values, first):
    field = lax.broadcasted_iota(jnp.int32, (2 * ROWS, LANES), 0) % ROWS
    lane = lax.broadcasted_iota(jnp.int32, (2 * ROWS, LANES), 1)
    row = jnp.zeros((2 * ROWS, LANES), F32)
    for k, value in enumerate(values):
        row = row + jnp.where(lane == (first + k) * ROWS + field, value, 0.0)
    return row


def second_rest_kernel(tiles, halo, offsets, start, vector, kept, matrices, outer, row, pairs):
    own, back, turned = views(matrices)
    for t in range(halo, tiles):
        put_pairs(pairs, t, vector[rows(t), :])
    for t in range(tiles, tiles + halo):
        pairs[t] = jnp.zeros((2 * ROWS, LANES), F32)
    for t in range(halo, tiles):
        value = here(t, pairs, own) + ahead(t, t + offsets[t], pairs, turned)
        outer[rows(t - halo), :] = kept[rows(t - halo), :] + value
    v0, v1 = start[...], vector[...]
    row[...] = placed((moment(v0, v0), moment(v0, v1), moment(v1, v1)), 0)


def third_kernel(tiles, halo, last, offsets, place, vector1, inner, outer, leaving, row, far, near, matrices, vector2, out, pairs, product):
    own, back, turned = views(matrices)
    flag = place[0] % 2
    put_rim(tiles, halo, flag, near, far, pairs)
    for t in range(halo):
        vector2[rows(t), :] = inner[rows(t), :] + select(flag, near[rows(t), :], far[rows(t), :])
    for t in range(halo, tiles):
        partner = jnp.maximum(t + offsets[t], halo)
        vector2[rows(t), :] = outer[rows(t - halo), :] + ahead(t, partner, pairs, turned)
    for t in range(tiles):
        put_pairs(pairs, t, vector2[rows(t), :])
    inside = jnp.where(place[0] == last, 0.0, 1.0).astype(F32)
    for t in range(halo):
        other = rows(halo + t)
        rim = select(flag, far[other, :], near[other, :]) + leaving[rows(t), :]
        put_pairs(pairs, tiles + t, rim * inside)
    for t in range(tiles):
        product[rows(t), :] = here(t, pairs, own) + 2.0 * ahead(t, t + offsets[t], pairs, turned)
    v1, v2, v3 = vector1[...], vector2[...], product[...]
    total = row[...] + placed((moment(v1, v2), moment(v2, v2), moment(v2, v3)), 3)
    total = jnp.sum(total, axis=0, keepdims=True)
    out[...] = jnp.broadcast_to(total[:, None, :], out.shape)


def last_kernel(tiles, moments, start, vector1, vector2, nodal, mixed):
    total = jnp.sum(moments[...], axis=0)
    total = jnp.broadcast_to(total, (2 * ROWS, LANES))
    g = [total if k == 0 else pltpu.roll(total, LANES - k * ROWS, 1) for k in range(MOMENTS)]
    h = [g[k + 1] + SHIFT * g[k] for k in range(MOMENTS - 1)]

    def form(table, c):
        n = len(c)
        result = None
        for i in range(n):
            for j in range(i, n):
                term = (c[i] * c[j]) * table[i + j]
                term = term if i == j else 2.0 * term
                result = term if result is None else result + term
        return result

    def apply(c):
        n = len(c)
        shifted = [SHIFT * c[0]]
        for i in range(1, n):
            shifted.append(c[i - 1] + SHIFT * c[i])
        return shifted + [c[n - 1]]

    one = jnp.ones_like(total)
    rr = g[0]
    alpha = rr / h[0]
    coefficients = [alpha]
    residual = [one - alpha * SHIFT, -alpha]
    new = form(g, residual)
    beta = new / rr
    direction = [residual[0] + beta, residual[1]]
    rr = new
    alpha = rr / form(h, direction)
    coefficients = [coefficients[0] + alpha * direction[0], alpha * direction[1]]
    image = apply(direction)
    residual = [residual[0] - alpha * image[0], residual[1] - alpha * image[1], -alpha * image[2]]
    new = form(g, residual)
    beta = new / rr
    direction = [residual[0] + beta * direction[0], residual[1] + beta * direction[1], residual[2]]
    rr = new
    alpha = rr / form(h, direction)
    coefficients = [
        coefficients[0] + alpha * direction[0],
        coefficients[1] + alpha * direction[1],
        alpha * direction[2],
    ]
    field = lax.broadcasted_iota(jnp.int32, (2 * ROWS, LANES), 0)
    lane = lax.broadcasted_iota(jnp.int32, (2 * ROWS, LANES), 1)
    result = jnp.zeros(start.shape, F32).reshape(-1, 2 * ROWS, LANES)
    for c, v in zip(coefficients, (start, vector1, vector2)):
        column = jnp.sum(jnp.where(lane == field % ROWS, c, 0.0), axis=1, keepdims=True)
        result = result + column[None] * v[...].reshape(-1, 2 * ROWS, LANES)
    mixed[...] = result.reshape(start.shape)
    for f in range(3):
        nodal[f] = mixed[pl.ds(f, tiles, stride=ROWS), :]


def call(kernel, shapes, smem, vmem, scratch, name, work=0):
    estimate = pl.CostEstimate(flops=work << 20, bytes_accessed=work << 16, transcendentals=0)
    return pl.pallas_call(
        kernel,
        out_shape=tuple(jax.ShapeDtypeStruct(s, F32) for s in shapes),
        in_specs=[SMEM] * len(smem) + [VMEM] * len(vmem),
        out_specs=tuple(VMEM for _ in shapes),
        scratch_shapes=scratch,
        compiler_params=pltpu.CompilerParams(vmem_limit_bytes=4 << 20),
        cost_estimate=estimate if work else None,
        name=name,
    )(*smem, *vmem)


def exchange(near, far, axis):
    n = lax.axis_size(axis)
    far_route = [(i, i + 1) for i in range(1, n - 1, 2)] + [(i + 1, i) for i in range(1, n - 1, 2)]
    near_route = [(i, i ^ 1) for i in range(n)]
    far = lax.ppermute(far, axis, far_route)
    near = lax.ppermute(near, axis, near_route)
    return near, far


def local(fluid_flux, margin_blocks, block_fluid, block_solid, diag_blocks, couple_blocks, couple_offset):
    owners = lax.axis_size("solid")
    groups = lax.axis_size("fluid")
    tiles = diag_blocks.shape[0]
    halo = tiles // 2
    total_blocks = block_fluid.shape[0]
    capacity = 5 * total_blocks // (2 * owners)
    chunk = capacity * 3 + ROWS
    place = lax.axis_index("solid").astype(jnp.int32).reshape(1)

    sent = margin(block_fluid, block_solid, fluid_flux, margin_blocks, owners, tiles, chunk)
    received = lax.all_to_all(sent, "solid", split_axis=0, concat_axis=0, tiled=True)
    matrices = prepare(diag_blocks, couple_blocks)
    part = combine(received, owners, tiles)
    parts = [part] + [
        lax.ppermute(part, "fluid", [(i, i ^ d) for i in range(groups)]) for d in (1, 2, 3)
    ]
    whole = (tiles * ROWS, LANES)
    half = (halo * ROWS, LANES)
    pairs = pltpu.VMEM((tiles + halo, 2 * ROWS, LANES), F32)
    spread = pltpu.VMEM((tiles + halo, ROWS, LANES), F32)
    start, kept, near, far = call(
        functools.partial(first_send_kernel, tiles, halo),
        (whole, half, half, half),
        (couple_offset, place),
        (*parts, matrices),
        [pairs, spread],
        "first_send",
    )
    near, far = exchange(near, far, "solid")
    mapped, image = call(
        functools.partial(first_rest_kernel, tiles, halo),
        ((3, tiles, LANES), whole),
        (couple_offset,),
        (start, kept, matrices),
        [pairs, pltpu.VMEM((tiles, ROWS, LANES), F32)],
        "first_rest",
        64,
    )
    vector1, inner, kept, leaving, near, far = call(
        functools.partial(second_send_kernel, tiles, halo),
        (whole, half, half, half, whole, whole),
        (couple_offset, place),
        (image, far, near, matrices),
        [pairs, spread],
        "second_send",
    )
    near, far = exchange(near, far, "solid")
    outer, row = call(
        functools.partial(second_rest_kernel, tiles, halo),
        (half, (2 * ROWS, LANES)),
        (couple_offset,),
        (start, vector1, kept, matrices),
        [pairs],
        "second_rest",
        64,
    )
    vector2, moments = call(
        functools.partial(third_kernel, tiles, halo, owners - 1),
        (whole, (owners, 1, LANES)),
        (couple_offset, place),
        (vector1, inner, outer, leaving, row, far, near, matrices),
        [pairs, pltpu.VMEM(whole, F32)],
        "third",
    )
    moments = lax.all_to_all(moments, "solid", split_axis=0, concat_axis=0, tiled=True)
    (nodal,) = call(
        functools.partial(last_kernel, tiles),
        ((3, tiles, LANES),),
        (),
        (moments, start, vector1, vector2),
        [pltpu.VMEM(whole, F32)],
        "last",
    )
    return mapped, nodal


def solution(mesh):
    in_specs = (
        P(None, ("fluid", "solid"), None),
        P(("fluid", "solid"), None, None),
        P(("fluid", "solid")),
        P(("fluid", "solid")),
        P("solid", None, None),
        P("solid", None, None),
        P("solid"),
    )
    out_specs = (P(None, "solid", None), P(None, "solid", None))
    return jax.shard_map(local, mesh=mesh, in_specs=in_specs, out_specs=out_specs, check_vma=False)
```

```python
import functools

import jax
import jax.numpy as jnp
from jax import lax
from jax.experimental import pallas as pl
from jax.experimental.pallas import tpu as pltpu
from jax.sharding import PartitionSpec as P

F32 = jnp.float32
BF16 = jnp.bfloat16
LANES = 128
ROWS = 4
SHIFT = 10.5
MOMENTS = 6
VMEM = pl.BlockSpec(memory_space=pltpu.VMEM)
SMEM = pl.BlockSpec(memory_space=pltpu.SMEM)
HBM = pl.BlockSpec(memory_space=pltpu.HBM)


def in_hbm(x):
    return pltpu.with_memory_space_constraint(x, pltpu.HBM)


def dot(a, b, contract=(1, 0)):
    return lax.dot_general(
        a, b, (((contract[0],), (contract[1],)), ((), ())), preferred_element_type=F32
    )


def split(x):
    high = x.astype(BF16).astype(F32)
    return high, x - high


def margin_kernel(owners, own_tiles, chunk, fluid_hbm, solid_hbm, flux_hbm, blocks_hbm, out, blocks, flux, left, right, fluid_ids, solid_ids, count, labels, sems):
    pieces = sems.shape[0] - 3
    size = blocks.shape[0] // pieces
    small = [
        pltpu.make_async_copy(source, target, sems.at[pieces + k])
        for k, (source, target) in enumerate(
            ((fluid_hbm, fluid_ids), (solid_hbm, solid_ids), (flux_hbm, flux))
        )
    ]

    def piece(k):
        part = pl.ds(k * size, size)
        return pltpu.make_async_copy(blocks_hbm.at[part], blocks.at[part], sems.at[k])

    for copy in small:
        copy.start()
    for k in range(pieces):
        piece(k).start()
    label_row = chunk - ROWS
    lane = lax.broadcasted_iota(jnp.int32, (1, LANES), 1)
    lane_first = jnp.where(lane < label_row, lane - lane % 3, -1)
    lane_field = lane % 3 * own_tiles
    out[...] = jnp.zeros_like(out)
    left[...] = jnp.zeros_like(left)
    right[...] = jnp.zeros_like(right)
    labels[...] = jnp.full_like(labels, -1.0)
    for owner in range(owners):
        count[owner] = 0
    for copy in small:
        copy.wait()
    for f in range(3):
        field = flux[f].astype(F32)
        left[pl.ds(f, flux.shape[1], stride=2 * ROWS), :] = field
        right[pl.ds(ROWS + f, flux.shape[1], stride=2 * ROWS), :] = field

    def place(block):
        solid = solid_ids[block]
        owner = lax.shift_right_logical(solid, own_tiles.bit_length() - 1)
        tile = solid & (own_tiles - 1)
        used = count[owner]
        count[owner] = used + 3
        label = (tile + lane_field).astype(F32)
        row = pl.ds(owner, 1)
        labels[row, :] = jnp.where(lane_first == used, label, labels[row, :])
        return owner * chunk + used

    def chosen(table, block):
        first = pl.multiple_of(fluid_ids[block] * (2 * ROWS), 2 * ROWS)
        return table[pl.ds(first, 2 * ROWS), :].astype(BF16)

    for k in range(pieces):
        piece(k).wait()
        for block in range(k * size, (k + 1) * size, 2):
            slots = place(block), place(block + 1)
            fields = jnp.concatenate([chosen(left, block), chosen(right, block + 1)], axis=1)
            terms = dot(fields, blocks[pl.ds(block, 2)].reshape(2 * LANES, LANES))
            for half, slot in enumerate(slots):
                for f in range(3):
                    row = half * ROWS + f
                    out[pl.ds(slot + f, 1), :] = terms[row : row + 1]
    for owner in range(owners):
        out[pl.ds(owner * chunk + label_row, 1), :] = labels[pl.ds(owner, 1), :]


def margin(fluid_ids, solid_ids, flux, blocks, owners, own_tiles, chunk):
    assert own_tiles & (own_tiles - 1) == 0
    pieces = 5
    assert blocks.shape[0] % (2 * pieces) == 0
    table = pltpu.VMEM((flux.shape[1] * 2 * ROWS, LANES), F32)
    return pl.pallas_call(
        functools.partial(margin_kernel, owners, own_tiles, chunk),
        out_shape=jax.ShapeDtypeStruct((owners * chunk, LANES), F32),
        in_specs=[HBM] * 4,
        out_specs=VMEM,
        scratch_shapes=[
            pltpu.VMEM(blocks.shape, BF16),
            pltpu.VMEM(flux.shape, BF16),
            table,
            table,
            pltpu.SMEM(fluid_ids.shape, jnp.int32),
            pltpu.SMEM(solid_ids.shape, jnp.int32),
            pltpu.SMEM((owners,), jnp.int32),
            pltpu.VMEM((owners, LANES), F32),
            pltpu.SemaphoreType.DMA((pieces + 3,)),
        ],
        compiler_params=pltpu.CompilerParams(vmem_limit_bytes=12 << 20),
        name="margin",
    )(*(in_hbm(x) for x in (fluid_ids, solid_ids, flux, blocks)))


def prepare_kernel(diag_hbm, couple_hbm, matrices, diag, couple, sems):
    pieces = sems.shape[1]
    size = diag.shape[0] // pieces

    def piece(k):
        part = pl.ds(k * size, size)
        return [
            pltpu.make_async_copy(source.at[part], target.at[part], sems.at[i, k])
            for i, (source, target) in enumerate(((diag_hbm, diag), (couple_hbm, couple)))
        ]

    for k in range(pieces):
        for copy in piece(k):
            copy.start()
    row = lax.broadcasted_iota(jnp.int32, (LANES, LANES), 0)
    column = lax.broadcasted_iota(jnp.int32, (LANES, LANES), 1)
    shift = jnp.where(row == column, SHIFT, 0.0).astype(F32)
    for k in range(pieces):
        for copy in piece(k):
            copy.wait()
        for t in range(k * size, (k + 1) * size):
            high, low = split(diag[t] - shift)
            matrices[t, 0:LANES, :] = high.astype(BF16)
            matrices[t, LANES : 2 * LANES, :] = low.astype(BF16)
            high, low = split(couple[t])
            matrices[t, 2 * LANES : 3 * LANES, :] = high.astype(BF16)
            matrices[t, 3 * LANES : 4 * LANES, :] = low.astype(BF16)
            matrices[t, 4 * LANES : 5 * LANES, :] = high.T.astype(BF16)
            matrices[t, 5 * LANES : 6 * LANES, :] = low.T.astype(BF16)


def prepare(diag, couple):
    tiles = diag.shape[0]
    return pl.pallas_call(
        prepare_kernel,
        out_shape=jax.ShapeDtypeStruct((tiles, 6 * LANES, LANES), BF16),
        in_specs=[HBM] * 2,
        out_specs=VMEM,
        scratch_shapes=[
            pltpu.VMEM(diag.shape, F32),
            pltpu.VMEM(couple.shape, F32),
            pltpu.SemaphoreType.DMA((2, 4)),
        ],
        compiler_params=pltpu.CompilerParams(vmem_limit_bytes=12 << 20),
        cost_estimate=pl.CostEstimate(flops=1 << 26, bytes_accessed=10 << 20, transcendentals=0),
        name="prepare",
    )(in_hbm(diag), in_hbm(couple))


def views(matrices):
    return tuple(matrices.at[:, 2 * k * LANES : 2 * (k + 1) * LANES, :] for k in range(3))


def combine_kernel(owners, received, out):
    chunk = received.shape[0] // owners
    row = lax.broadcasted_iota(jnp.int32, (out.shape[0], chunk), 0).astype(F32)
    total = jnp.zeros(out.shape, F32)
    for source in range(owners):
        values = received[source * chunk : (source + 1) * chunk, :]
        label = received[(source + 1) * chunk - ROWS : (source + 1) * chunk - ROWS + 1, 0:chunk]
        hits = (row == label).astype(F32).astype(BF16)
        high, low = split(values)
        total = total + dot(hits, high.astype(BF16)) + dot(hits, low.astype(BF16))
    out[...] = total


def combine(received, owners, own_tiles):
    return pl.pallas_call(
        functools.partial(combine_kernel, owners),
        out_shape=jax.ShapeDtypeStruct((own_tiles * 3, LANES), F32),
        in_specs=[VMEM],
        out_specs=VMEM,
        compiler_params=pltpu.CompilerParams(vmem_limit_bytes=16 << 20),
        name="combine",
    )(received)


def put_pairs(pairs, t, value):
    high, low = split(value)
    pairs[t, 0:ROWS, :] = high
    pairs[t, ROWS : 2 * ROWS, :] = low


def load_pairs(pairs, t):
    both = pairs[t].astype(BF16)
    return jnp.concatenate([both, both], axis=1)


def fold(product):
    return product[0:ROWS] + product[ROWS : 2 * ROWS]


def ahead(t, partner, pairs, turned):
    return fold(dot(load_pairs(pairs, partner), turned[t]))


def here(t, pairs, matrix):
    return fold(dot(load_pairs(pairs, t), matrix[t]))


def rows(t, count=1):
    return slice(t * ROWS, (t + count) * ROWS)


def select(flag, first, second):
    return jnp.where(flag > 0, first, second)


def add_transposed(tiles, offsets, pairs, spread, back, products, first, stop):
    for t in range(first, stop):
        products[t] = here(t, pairs, back)
    for t in range(first, stop):
        partner = t + offsets[t]
        spread[partner] = spread[partner] + products[t]


def first_send_kernel(tiles, halo, offsets, place, part0, part1, part3, part2, matrices, vector, kept, near, far, pairs, spread, products):
    own, back, turned = views(matrices)
    total = (part0[...] + part1[...]) + (part2[...] + part3[...])
    for f in range(3):
        vector[pl.ds(f, tiles, stride=ROWS), :] = total[f * tiles : (f + 1) * tiles]
    vector[pl.ds(3, tiles, stride=ROWS), :] = jnp.zeros((tiles, LANES), F32)
    for t in range(halo, tiles):
        put_pairs(pairs, t, vector[rows(t), :])
    spread[...] = jnp.zeros_like(spread)
    add_transposed(tiles, offsets, pairs, spread, back, products, halo, tiles)
    flag = place[0] % 2
    for t in range(halo):
        rim = vector[rows(t), :]
        out = spread[tiles + t]
        near[rows(t), :] = select(flag, rim, out)
        far[rows(t), :] = select(flag, out, rim)
        kept[rows(t), :] = spread[halo + t]


def first_rest_kernel(tiles, halo, offsets, vector, kept, matrices, mapped, image, pairs, spread, products):
    own, back, turned = views(matrices)
    for f in range(3):
        mapped[f] = vector[pl.ds(f, tiles, stride=ROWS), :]
    for t in range(tiles):
        put_pairs(pairs, t, vector[rows(t), :])
    for t in range(tiles, tiles + halo):
        pairs[t] = jnp.zeros((2 * ROWS, LANES), F32)
    for t in range(halo):
        spread[t] = jnp.zeros((ROWS, LANES), F32)
        spread[halo + t] = kept[rows(t), :]
    add_transposed(tiles, offsets, pairs, spread, back, products, 0, halo)
    for t in range(tiles):
        value = here(t, pairs, own) + ahead(t, t + offsets[t], pairs, turned)
        image[rows(t), :] = spread[t] + value


def put_rim(tiles, halo, flag, near, far, pairs):
    for t in range(halo):
        put_pairs(pairs, tiles + t, select(flag, far[rows(t), :], near[rows(t), :]))
        pairs[tiles - halo + t] = jnp.zeros((2 * ROWS, LANES), F32)


def second_send_kernel(tiles, halo, offsets, place, image, far, near, matrices, vector, inner, kept, leaving, near2, far2, pairs, spread, products):
    own, back, turned = views(matrices)
    flag = place[0] % 2
    put_rim(tiles, halo, flag, near, far, pairs)
    for t in range(halo):
        vector[rows(t), :] = image[rows(t), :] + select(flag, near[rows(t), :], far[rows(t), :])
    for t in range(halo, tiles):
        partner = jnp.maximum(t + offsets[t], halo)
        vector[rows(t), :] = image[rows(t), :] + ahead(t, partner, pairs, turned)
    for t in range(tiles):
        put_pairs(pairs, t, vector[rows(t), :])
    spread[...] = jnp.zeros_like(spread)
    add_transposed(tiles, offsets, pairs, spread, back, products, 0, tiles)
    size = halo * ROWS
    for t in range(halo):
        inner[rows(t), :] = spread[t] + (here(t, pairs, own) + ahead(t, t + offsets[t], pairs, turned))
        kept[rows(t), :] = spread[halo + t]
        leaving[rows(t), :] = spread[tiles + t]
    near2[0:size, :] = select(flag, vector[0:size, :], leaving[...])
    far2[0:size, :] = select(flag, leaving[...], vector[0:size, :])
    near2[size : 2 * size, :] = inner[...]
    far2[size : 2 * size, :] = inner[...]


def moment(a, b):
    folded = jnp.sum((a * b).reshape(-1, 2 * ROWS, LANES), axis=0)
    return jnp.sum(folded, axis=1, keepdims=True)


def placed(values, first):
    field = lax.broadcasted_iota(jnp.int32, (2 * ROWS, LANES), 0) % ROWS
    lane = lax.broadcasted_iota(jnp.int32, (2 * ROWS, LANES), 1)
    row = jnp.zeros((2 * ROWS, LANES), F32)
    for k, value in enumerate(values):
        row = row + jnp.where(lane == (first + k) * ROWS + field, value, 0.0)
    return row


def second_rest_kernel(tiles, halo, offsets, start, vector, kept, matrices, outer, row, pairs):
    own, back, turned = views(matrices)
    for t in range(halo, tiles):
        put_pairs(pairs, t, vector[rows(t), :])
    for t in range(tiles, tiles + halo):
        pairs[t] = jnp.zeros((2 * ROWS, LANES), F32)
    for t in range(halo, tiles):
        value = here(t, pairs, own) + ahead(t, t + offsets[t], pairs, turned)
        outer[rows(t - halo), :] = kept[rows(t - halo), :] + value
    v0, v1 = start[...], vector[...]
    row[...] = placed((moment(v0, v0), moment(v0, v1), moment(v1, v1)), 0)


def third_kernel(tiles, halo, last, offsets, place, vector1, inner, outer, leaving, row, far, near, matrices, vector2, out, pairs, product):
    own, back, turned = views(matrices)
    flag = place[0] % 2
    put_rim(tiles, halo, flag, near, far, pairs)
    for t in range(halo):
        vector2[rows(t), :] = inner[rows(t), :] + select(flag, near[rows(t), :], far[rows(t), :])
    for t in range(halo, tiles):
        partner = jnp.maximum(t + offsets[t], halo)
        vector2[rows(t), :] = outer[rows(t - halo), :] + ahead(t, partner, pairs, turned)
    for t in range(tiles):
        put_pairs(pairs, t, vector2[rows(t), :])
    inside = jnp.where(place[0] == last, 0.0, 1.0).astype(F32)
    for t in range(halo):
        other = rows(halo + t)
        rim = select(flag, far[other, :], near[other, :]) + leaving[rows(t), :]
        put_pairs(pairs, tiles + t, rim * inside)
    for t in range(tiles):
        product[rows(t), :] = here(t, pairs, own) + 2.0 * ahead(t, t + offsets[t], pairs, turned)
    v1, v2, v3 = vector1[...], vector2[...], product[...]
    total = row[...] + placed((moment(v1, v2), moment(v2, v2), moment(v2, v3)), 3)
    total = jnp.sum(total, axis=0, keepdims=True)
    out[...] = jnp.broadcast_to(total[:, None, :], out.shape)


def last_kernel(tiles, moments, start, vector1, vector2, nodal, mixed):
    total = jnp.sum(moments[...], axis=0)
    total = jnp.broadcast_to(total, (2 * ROWS, LANES))
    g = [total if k == 0 else pltpu.roll(total, LANES - k * ROWS, 1) for k in range(MOMENTS)]
    h = [g[k + 1] + SHIFT * g[k] for k in range(MOMENTS - 1)]

    def form(table, c):
        n = len(c)
        result = None
        for i in range(n):
            for j in range(i, n):
                term = (c[i] * c[j]) * table[i + j]
                term = term if i == j else 2.0 * term
                result = term if result is None else result + term
        return result

    def apply(c):
        n = len(c)
        shifted = [SHIFT * c[0]]
        for i in range(1, n):
            shifted.append(c[i - 1] + SHIFT * c[i])
        return shifted + [c[n - 1]]

    one = jnp.ones_like(total)
    rr = g[0]
    alpha = rr / h[0]
    coefficients = [alpha]
    residual = [one - alpha * SHIFT, -alpha]
    new = form(g, residual)
    beta = new / rr
    direction = [residual[0] + beta, residual[1]]
    rr = new
    alpha = rr / form(h, direction)
    coefficients = [coefficients[0] + alpha * direction[0], alpha * direction[1]]
    image = apply(direction)
    residual = [residual[0] - alpha * image[0], residual[1] - alpha * image[1], -alpha * image[2]]
    new = form(g, residual)
    beta = new / rr
    direction = [residual[0] + beta * direction[0], residual[1] + beta * direction[1], residual[2]]
    rr = new
    alpha = rr / form(h, direction)
    coefficients = [
        coefficients[0] + alpha * direction[0],
        coefficients[1] + alpha * direction[1],
        alpha * direction[2],
    ]
    field = lax.broadcasted_iota(jnp.int32, (2 * ROWS, LANES), 0)
    lane = lax.broadcasted_iota(jnp.int32, (2 * ROWS, LANES), 1)
    result = jnp.zeros(start.shape, F32).reshape(-1, 2 * ROWS, LANES)
    for c, v in zip(coefficients, (start, vector1, vector2)):
        column = jnp.sum(jnp.where(lane == field % ROWS, c, 0.0), axis=1, keepdims=True)
        result = result + column[None] * v[...].reshape(-1, 2 * ROWS, LANES)
    mixed[...] = result.reshape(start.shape)
    for f in range(3):
        nodal[f] = mixed[pl.ds(f, tiles, stride=ROWS), :]


def call(kernel, shapes, smem, vmem, scratch, name, work=0):
    estimate = pl.CostEstimate(flops=work << 20, bytes_accessed=work << 16, transcendentals=0)
    return pl.pallas_call(
        kernel,
        out_shape=tuple(jax.ShapeDtypeStruct(s, F32) for s in shapes),
        in_specs=[SMEM] * len(smem) + [VMEM] * len(vmem),
        out_specs=tuple(VMEM for _ in shapes),
        scratch_shapes=scratch,
        compiler_params=pltpu.CompilerParams(vmem_limit_bytes=4 << 20),
        cost_estimate=estimate if work else None,
        name=name,
    )(*smem, *vmem)


def exchange(near, far, axis):
    n = lax.axis_size(axis)
    far_route = [(i, i + 1) for i in range(1, n - 1, 2)] + [(i + 1, i) for i in range(1, n - 1, 2)]
    near_route = [(i, i ^ 1) for i in range(n)]
    far = lax.ppermute(far, axis, far_route)
    near = lax.ppermute(near, axis, near_route)
    return near, far


def local(fluid_flux, margin_blocks, block_fluid, block_solid, diag_blocks, couple_blocks, couple_offset):
    owners = lax.axis_size("solid")
    groups = lax.axis_size("fluid")
    tiles = diag_blocks.shape[0]
    halo = tiles // 2
    total_blocks = block_fluid.shape[0]
    capacity = 5 * total_blocks // (2 * owners)
    chunk = capacity * 3 + ROWS
    place = lax.axis_index("solid").astype(jnp.int32).reshape(1)

    sent = margin(block_fluid, block_solid, fluid_flux, margin_blocks, owners, tiles, chunk)
    received = lax.all_to_all(sent, "solid", split_axis=0, concat_axis=0, tiled=True)
    matrices = prepare(diag_blocks, couple_blocks)
    part = combine(received, owners, tiles)
    part1, part2, part3 = (
        lax.ppermute(part, "fluid", [(i, i ^ d) for i in range(groups)]) for d in (1, 2, 3)
    )
    whole = (tiles * ROWS, LANES)
    half = (halo * ROWS, LANES)
    pairs = pltpu.VMEM((tiles + halo, 2 * ROWS, LANES), F32)
    spread = pltpu.VMEM((tiles + halo, ROWS, LANES), F32)
    products = pltpu.VMEM((tiles, ROWS, LANES), F32)
    start, kept, near, far = call(
        functools.partial(first_send_kernel, tiles, halo),
        (whole, half, half, half),
        (couple_offset, place),
        (part, part1, part3, part2, matrices),
        [pairs, spread, products],
        "first_send",
    )
    near, far = exchange(near, far, "solid")
    mapped, image = call(
        functools.partial(first_rest_kernel, tiles, halo),
        ((3, tiles, LANES), whole),
        (couple_offset,),
        (start, kept, matrices),
        [pairs, products, products],
        "first_rest",
        64,
    )
    vector1, inner, kept, leaving, near, far = call(
        functools.partial(second_send_kernel, tiles, halo),
        (whole, half, half, half, whole, whole),
        (couple_offset, place),
        (image, far, near, matrices),
        [pairs, spread, products],
        "second_send",
    )
    near, far = exchange(near, far, "solid")
    outer, row = call(
        functools.partial(second_rest_kernel, tiles, halo),
        (half, (2 * ROWS, LANES)),
        (couple_offset,),
        (start, vector1, kept, matrices),
        [pairs],
        "second_rest",
        64,
    )
    vector2, moments = call(
        functools.partial(third_kernel, tiles, halo, owners - 1),
        (whole, (owners, 1, LANES)),
        (couple_offset, place),
        (vector1, inner, outer, leaving, row, far, near, matrices),
        [pairs, pltpu.VMEM(whole, F32)],
        "third",
    )
    moments = lax.all_to_all(moments, "solid", split_axis=0, concat_axis=0, tiled=True)
    (nodal,) = call(
        functools.partial(last_kernel, tiles),
        ((3, tiles, LANES),),
        (),
        (moments, start, vector1, vector2),
        [pltpu.VMEM(whole, F32)],
        "last",
    )
    return mapped, nodal


def solution(mesh):
    in_specs = (
        P(None, ("fluid", "solid"), None),
        P(("fluid", "solid"), None, None),
        P(("fluid", "solid")),
        P(("fluid", "solid")),
        P("solid", None, None),
        P("solid", None, None),
        P("solid"),
    )
    out_specs = (P(None, "solid", None), P(None, "solid", None))
    return jax.shard_map(local, mesh=mesh, in_specs=in_specs, out_specs=out_specs, check_vma=False)
```

```python
import functools

import jax
import jax.numpy as jnp
from jax import lax
from jax.experimental import pallas as pl
from jax.experimental.pallas import tpu as pltpu
from jax.sharding import PartitionSpec as P

F32 = jnp.float32
BF16 = jnp.bfloat16
LANES = 128
ROWS = 4
SHIFT = 10.5
MOMENTS = 6
VMEM = pl.BlockSpec(memory_space=pltpu.VMEM)
SMEM = pl.BlockSpec(memory_space=pltpu.SMEM)
HBM = pl.BlockSpec(memory_space=pltpu.HBM)


def in_hbm(x):
    return pltpu.with_memory_space_constraint(x, pltpu.HBM)


def dot(a, b, contract=(1, 0)):
    return lax.dot_general(
        a, b, (((contract[0],), (contract[1],)), ((), ())), preferred_element_type=F32
    )


def split(x):
    high = x.astype(BF16).astype(F32)
    return high, x - high


def margin_kernel(owners, own_tiles, chunk, fluid_hbm, solid_hbm, flux_hbm, blocks_hbm, out, blocks, flux, left, right, fluid_ids, solid_ids, count, labels, sems):
    pieces = sems.shape[0] - 3
    size = blocks.shape[0] // pieces
    small = [
        pltpu.make_async_copy(source, target, sems.at[pieces + k])
        for k, (source, target) in enumerate(
            ((fluid_hbm, fluid_ids), (solid_hbm, solid_ids), (flux_hbm, flux))
        )
    ]

    def piece(k):
        part = pl.ds(k * size, size)
        return pltpu.make_async_copy(blocks_hbm.at[part], blocks.at[part], sems.at[k])

    for copy in small:
        copy.start()
    for k in range(pieces):
        piece(k).start()
    label_row = chunk - ROWS
    lane = lax.broadcasted_iota(jnp.int32, (1, LANES), 1)
    lane_first = jnp.where(lane < label_row, lane - lane % 3, -1)
    lane_field = lane % 3 * own_tiles
    out[...] = jnp.zeros_like(out)
    left[...] = jnp.zeros_like(left)
    right[...] = jnp.zeros_like(right)
    labels[...] = jnp.full_like(labels, -1.0)
    for owner in range(owners):
        count[owner] = 0
    for copy in small:
        copy.wait()
    for f in range(3):
        field = flux[f].astype(F32)
        left[pl.ds(f, flux.shape[1], stride=2 * ROWS), :] = field
        right[pl.ds(ROWS + f, flux.shape[1], stride=2 * ROWS), :] = field

    def place(block):
        solid = solid_ids[block]
        owner = lax.shift_right_logical(solid, own_tiles.bit_length() - 1)
        tile = solid & (own_tiles - 1)
        used = count[owner]
        count[owner] = used + 3
        label = (tile + lane_field).astype(F32)
        row = pl.ds(owner, 1)
        labels[row, :] = jnp.where(lane_first == used, label, labels[row, :])
        return owner * chunk + used

    def chosen(table, block):
        first = pl.multiple_of(fluid_ids[block] * (2 * ROWS), 2 * ROWS)
        return table[pl.ds(first, 2 * ROWS), :].astype(BF16)

    for k in range(pieces):
        piece(k).wait()
        for block in range(k * size, (k + 1) * size, 2):
            slots = place(block), place(block + 1)
            fields = jnp.concatenate([chosen(left, block), chosen(right, block + 1)], axis=1)
            terms = dot(fields, blocks[pl.ds(block, 2)].reshape(2 * LANES, LANES))
            for half, slot in enumerate(slots):
                for f in range(3):
                    row = half * ROWS + f
                    out[pl.ds(slot + f, 1), :] = terms[row : row + 1]
    for owner in range(owners):
        out[pl.ds(owner * chunk + label_row, 1), :] = labels[pl.ds(owner, 1), :]


def margin(fluid_ids, solid_ids, flux, blocks, owners, own_tiles, chunk):
    assert own_tiles & (own_tiles - 1) == 0
    pieces = 5
    assert blocks.shape[0] % (2 * pieces) == 0
    table = pltpu.VMEM((flux.shape[1] * 2 * ROWS, LANES), F32)
    return pl.pallas_call(
        functools.partial(margin_kernel, owners, own_tiles, chunk),
        out_shape=jax.ShapeDtypeStruct((owners * chunk, LANES), F32),
        in_specs=[HBM] * 4,
        out_specs=VMEM,
        scratch_shapes=[
            pltpu.VMEM(blocks.shape, BF16),
            pltpu.VMEM(flux.shape, BF16),
            table,
            table,
            pltpu.SMEM(fluid_ids.shape, jnp.int32),
            pltpu.SMEM(solid_ids.shape, jnp.int32),
            pltpu.SMEM((owners,), jnp.int32),
            pltpu.VMEM((owners, LANES), F32),
            pltpu.SemaphoreType.DMA((pieces + 3,)),
        ],
        compiler_params=pltpu.CompilerParams(vmem_limit_bytes=12 << 20),
        name="margin",
    )(*(in_hbm(x) for x in (fluid_ids, solid_ids, flux, blocks)))


def prepare_kernel(diag_hbm, couple_hbm, matrices, diag, couple, sems):
    pieces = sems.shape[1]
    size = diag.shape[0] // pieces

    def piece(k):
        part = pl.ds(k * size, size)
        return [
            pltpu.make_async_copy(source.at[part], target.at[part], sems.at[i, k])
            for i, (source, target) in enumerate(((diag_hbm, diag), (couple_hbm, couple)))
        ]

    for k in range(pieces):
        for copy in piece(k):
            copy.start()
    row = lax.broadcasted_iota(jnp.int32, (LANES, LANES), 0)
    column = lax.broadcasted_iota(jnp.int32, (LANES, LANES), 1)
    shift = jnp.where(row == column, SHIFT, 0.0).astype(F32)
    for k in range(pieces):
        for copy in piece(k):
            copy.wait()
        for t in range(k * size, (k + 1) * size):
            high, low = split(diag[t] - shift)
            matrices[t, 0:LANES, :] = high.astype(BF16)
            matrices[t, LANES : 2 * LANES, :] = low.astype(BF16)
            high, low = split(couple[t])
            matrices[t, 2 * LANES : 3 * LANES, :] = high.astype(BF16)
            matrices[t, 3 * LANES : 4 * LANES, :] = low.astype(BF16)
            matrices[t, 4 * LANES : 5 * LANES, :] = high.T.astype(BF16)
            matrices[t, 5 * LANES : 6 * LANES, :] = low.T.astype(BF16)


def prepare(diag, couple):
    tiles = diag.shape[0]
    return pl.pallas_call(
        prepare_kernel,
        out_shape=jax.ShapeDtypeStruct((tiles, 6 * LANES, LANES), BF16),
        in_specs=[HBM] * 2,
        out_specs=VMEM,
        scratch_shapes=[
            pltpu.VMEM(diag.shape, F32),
            pltpu.VMEM(couple.shape, F32),
            pltpu.SemaphoreType.DMA((2, 4)),
        ],
        compiler_params=pltpu.CompilerParams(vmem_limit_bytes=12 << 20),
        cost_estimate=pl.CostEstimate(flops=1 << 26, bytes_accessed=10 << 20, transcendentals=0),
        name="prepare",
    )(in_hbm(diag), in_hbm(couple))


def views(matrices):
    return tuple(matrices.at[:, 2 * k * LANES : 2 * (k + 1) * LANES, :] for k in range(3))


def combine_kernel(owners, received, out):
    chunk = received.shape[0] // owners
    row = lax.broadcasted_iota(jnp.int32, (out.shape[0], chunk), 0).astype(F32)
    total = jnp.zeros(out.shape, F32)
    for source in range(owners):
        values = received[source * chunk : (source + 1) * chunk, :]
        label = received[(source + 1) * chunk - ROWS : (source + 1) * chunk - ROWS + 1, 0:chunk]
        hits = (row == label).astype(F32).astype(BF16)
        high, low = split(values)
        total = total + dot(hits, high.astype(BF16)) + dot(hits, low.astype(BF16))
    out[...] = total


def combine(received, owners, own_tiles):
    return pl.pallas_call(
        functools.partial(combine_kernel, owners),
        out_shape=jax.ShapeDtypeStruct((own_tiles * 3, LANES), F32),
        in_specs=[VMEM],
        out_specs=VMEM,
        compiler_params=pltpu.CompilerParams(vmem_limit_bytes=16 << 20),
        name="combine",
    )(received)


def put_pairs(pairs, t, value):
    high, low = split(value)
    pairs[t, 0:ROWS, :] = high
    pairs[t, ROWS : 2 * ROWS, :] = low


def load_pairs(pairs, t):
    both = pairs[t].astype(BF16)
    return jnp.concatenate([both, both], axis=1)


def fold(product):
    return product[0:ROWS] + product[ROWS : 2 * ROWS]


def ahead(t, partner, pairs, turned):
    return fold(dot(load_pairs(pairs, partner), turned[t]))


def here(t, pairs, matrix):
    return fold(dot(load_pairs(pairs, t), matrix[t]))


def rows(t, count=1):
    return slice(t * ROWS, (t + count) * ROWS)


def select(flag, first, second):
    return jnp.where(flag > 0, first, second)


def add_transposed(tiles, arrived, pairs, spread, back, products, first, stop):
    for t in range(first, stop):
        products[t] = here(t, pairs, back)
    offsets = arrived()
    for t in range(first, stop):
        partner = t + offsets[t]
        spread[partner] = spread[partner] + products[t]


def first_send_kernel(tiles, halo, arrived, part0, part1, part3, part2, matrices, vector, kept, near, far, pairs, spread, products):
    own, back, turned = views(matrices)
    total = (part0[...] + part1[...]) + (part2[...] + part3[...])
    for f in range(3):
        vector[pl.ds(f, tiles, stride=ROWS), :] = total[f * tiles : (f + 1) * tiles]
    vector[pl.ds(3, tiles, stride=ROWS), :] = jnp.zeros((tiles, LANES), F32)
    for t in range(halo, tiles):
        put_pairs(pairs, t, vector[rows(t), :])
    spread[...] = jnp.zeros_like(spread)
    add_transposed(tiles, arrived, pairs, spread, back, products, halo, tiles)
    flag = lax.axis_index("solid") % 2
    for t in range(halo):
        rim = vector[rows(t), :]
        out = spread[tiles + t]
        near[rows(t), :] = select(flag, rim, out)
        far[rows(t), :] = select(flag, out, rim)
        kept[rows(t), :] = spread[halo + t]


def first_rest_kernel(tiles, halo, arrived, vector, kept, matrices, mapped, image, pairs, spread, products):
    own, back, turned = views(matrices)
    for f in range(3):
        mapped[f] = vector[pl.ds(f, tiles, stride=ROWS), :]
    for t in range(tiles):
        put_pairs(pairs, t, vector[rows(t), :])
    for t in range(tiles, tiles + halo):
        pairs[t] = jnp.zeros((2 * ROWS, LANES), F32)
    for t in range(halo):
        spread[t] = jnp.zeros((ROWS, LANES), F32)
        spread[halo + t] = kept[rows(t), :]
    offsets = arrived()
    add_transposed(tiles, lambda: offsets, pairs, spread, back, products, 0, halo)
    for t in range(tiles):
        value = here(t, pairs, own) + ahead(t, t + offsets[t], pairs, turned)
        image[rows(t), :] = spread[t] + value


def put_rim(tiles, halo, flag, near, far, pairs):
    for t in range(halo):
        put_pairs(pairs, tiles + t, select(flag, far[rows(t), :], near[rows(t), :]))
        pairs[tiles - halo + t] = jnp.zeros((2 * ROWS, LANES), F32)


def second_send_kernel(tiles, halo, arrived, image, far, near, matrices, vector, inner, kept, leaving, near2, far2, pairs, spread, products):
    own, back, turned = views(matrices)
    flag = lax.axis_index("solid") % 2
    put_rim(tiles, halo, flag, near, far, pairs)
    offsets = arrived()
    for t in range(halo):
        vector[rows(t), :] = image[rows(t), :] + select(flag, near[rows(t), :], far[rows(t), :])
    for t in range(halo, tiles):
        partner = jnp.maximum(t + offsets[t], halo)
        vector[rows(t), :] = image[rows(t), :] + ahead(t, partner, pairs, turned)
    for t in range(tiles):
        put_pairs(pairs, t, vector[rows(t), :])
    spread[...] = jnp.zeros_like(spread)
    add_transposed(tiles, lambda: offsets, pairs, spread, back, products, 0, tiles)
    size = halo * ROWS
    for t in range(halo):
        inner[rows(t), :] = spread[t] + (here(t, pairs, own) + ahead(t, t + offsets[t], pairs, turned))
        kept[rows(t), :] = spread[halo + t]
        leaving[rows(t), :] = spread[tiles + t]
    near2[0:size, :] = select(flag, vector[0:size, :], leaving[...])
    far2[0:size, :] = select(flag, leaving[...], vector[0:size, :])
    near2[size : 2 * size, :] = inner[...]
    far2[size : 2 * size, :] = inner[...]


def moment(a, b):
    folded = jnp.sum((a * b).reshape(-1, 2 * ROWS, LANES), axis=0)
    return jnp.sum(folded, axis=1, keepdims=True)


def placed(values, first):
    field = lax.broadcasted_iota(jnp.int32, (2 * ROWS, LANES), 0) % ROWS
    lane = lax.broadcasted_iota(jnp.int32, (2 * ROWS, LANES), 1)
    row = jnp.zeros((2 * ROWS, LANES), F32)
    for k, value in enumerate(values):
        row = row + jnp.where(lane == (first + k) * ROWS + field, value, 0.0)
    return row


def second_rest_kernel(tiles, halo, arrived, start, vector, kept, matrices, outer, row, pairs):
    own, back, turned = views(matrices)
    for t in range(halo, tiles):
        put_pairs(pairs, t, vector[rows(t), :])
    for t in range(tiles, tiles + halo):
        pairs[t] = jnp.zeros((2 * ROWS, LANES), F32)
    offsets = arrived()
    for t in range(halo, tiles):
        value = here(t, pairs, own) + ahead(t, t + offsets[t], pairs, turned)
        outer[rows(t - halo), :] = kept[rows(t - halo), :] + value
    v0, v1 = start[...], vector[...]
    row[...] = placed((moment(v0, v0), moment(v0, v1), moment(v1, v1)), 0)


def third_kernel(tiles, halo, last, arrived, vector1, inner, outer, leaving, row, far, near, matrices, vector2, out, pairs):
    own, back, turned = views(matrices)
    flag = lax.axis_index("solid") % 2
    put_rim(tiles, halo, flag, near, far, pairs)
    offsets = arrived()
    outside = [
        ahead(t, jnp.maximum(t + offsets[t], halo), pairs, turned) for t in range(halo, tiles)
    ]
    size = halo * ROWS
    vector2[0:size, :] = inner[...] + select(flag, near[0:size, :], far[0:size, :])
    for t in range(halo):
        put_pairs(pairs, t, vector2[rows(t), :])
    quadratic = jnp.zeros((ROWS, LANES), F32)
    for t in range(halo):
        quadratic = quadratic + vector2[rows(t), :] * here(t, pairs, own)
    for t in range(halo, tiles):
        value = outer[rows(t - halo), :] + outside[t - halo]
        vector2[rows(t), :] = value
        put_pairs(pairs, t, value)
    inside = jnp.where(lax.axis_index("solid") == last, 0.0, 1.0).astype(F32)
    for t in range(halo):
        other = rows(halo + t)
        rim = select(flag, far[other, :], near[other, :]) + leaving[rows(t), :]
        put_pairs(pairs, tiles + t, rim * inside)
    for t in range(halo, tiles):
        quadratic = quadratic + vector2[rows(t), :] * here(t, pairs, own)
    v1, v2 = vector1[...], vector2[...]
    total = row[...] + placed((moment(v1, v2), moment(v2, v2)), 3)
    coupled = jnp.zeros((ROWS, LANES), F32)
    for t in range(tiles):
        coupled = coupled + vector2[rows(t), :] * ahead(t, t + offsets[t], pairs, turned)
    quadratic = jnp.sum(quadratic + 2.0 * coupled, axis=1, keepdims=True)
    quadratic = jnp.concatenate([quadratic, jnp.zeros((ROWS, 1), F32)], axis=0)
    total = total + placed((quadratic,), 5)
    total = jnp.sum(total, axis=0, keepdims=True)
    out[...] = jnp.broadcast_to(total, out.shape)


def last_kernel(tiles, moments, start, vector1, vector2, nodal, mixed):
    total = jnp.sum(moments[...].reshape(-1, 2 * ROWS, LANES), axis=0)
    total = jnp.broadcast_to(jnp.sum(total, axis=0, keepdims=True), total.shape)
    g = [total if k == 0 else pltpu.roll(total, LANES - k * ROWS, 1) for k in range(MOMENTS)]
    h = [g[k + 1] + SHIFT * g[k] for k in range(MOMENTS - 1)]

    def form(table, c):
        n = len(c)
        result = None
        for i in range(n):
            for j in range(i, n):
                term = (c[i] * c[j]) * table[i + j]
                term = term if i == j else 2.0 * term
                result = term if result is None else result + term
        return result

    def apply(c):
        n = len(c)
        shifted = [SHIFT * c[0]]
        for i in range(1, n):
            shifted.append(c[i - 1] + SHIFT * c[i])
        return shifted + [c[n - 1]]

    one = jnp.ones_like(total)
    rr = g[0]
    alpha = rr / h[0]
    coefficients = [alpha]
    residual = [one - alpha * SHIFT, -alpha]
    new = form(g, residual)
    beta = new / rr
    direction = [residual[0] + beta, residual[1]]
    rr = new
    alpha = rr / form(h, direction)
    coefficients = [coefficients[0] + alpha * direction[0], alpha * direction[1]]
    image = apply(direction)
    residual = [residual[0] - alpha * image[0], residual[1] - alpha * image[1], -alpha * image[2]]
    new = form(g, residual)
    beta = new / rr
    direction = [residual[0] + beta * direction[0], residual[1] + beta * direction[1], residual[2]]
    rr = new
    alpha = rr / form(h, direction)
    coefficients = [
        coefficients[0] + alpha * direction[0],
        coefficients[1] + alpha * direction[1],
        alpha * direction[2],
    ]
    field = lax.broadcasted_iota(jnp.int32, (2 * ROWS, LANES), 0)
    lane = lax.broadcasted_iota(jnp.int32, (2 * ROWS, LANES), 1)
    result = jnp.zeros(start.shape, F32).reshape(-1, 2 * ROWS, LANES)
    for c, v in zip(coefficients, (start, vector1, vector2)):
        column = jnp.sum(jnp.where(lane == field % ROWS, c, 0.0), axis=1, keepdims=True)
        result = result + column[None] * v[...].reshape(-1, 2 * ROWS, LANES)
    mixed[...] = result.reshape(start.shape)
    for f in range(3):
        nodal[f] = mixed[pl.ds(f, tiles, stride=ROWS), :]


def with_offsets(kernel):
    def run(source, *refs):
        *refs, offsets, sem = refs
        copy = pltpu.make_async_copy(source, offsets, sem)
        copy.start()

        def arrived():
            copy.wait()
            return offsets

        kernel(arrived, *refs)

    return run


def call(kernel, shapes, offsets, vmem, scratch, name, work=0):
    estimate = pl.CostEstimate(flops=work << 20, bytes_accessed=work << 16, transcendentals=0)
    return pl.pallas_call(
        with_offsets(kernel),
        out_shape=tuple(jax.ShapeDtypeStruct(s, F32) for s in shapes),
        in_specs=[pl.BlockSpec(memory_space=pl.ANY)] + [VMEM] * len(vmem),
        out_specs=tuple(VMEM for _ in shapes),
        scratch_shapes=[
            *scratch,
            pltpu.SMEM(offsets.shape, jnp.int32),
            pltpu.SemaphoreType.DMA(()),
        ],
        compiler_params=pltpu.CompilerParams(vmem_limit_bytes=4 << 20),
        cost_estimate=estimate if work else None,
        name=name,
    )(offsets, *vmem)


def exchange(near, far, axis):
    n = lax.axis_size(axis)
    far_route = [(i, i + 1) for i in range(1, n - 1, 2)] + [(i + 1, i) for i in range(1, n - 1, 2)]
    near_route = [(i, i ^ 1) for i in range(n)]
    far = lax.ppermute(far, axis, far_route)
    near = lax.ppermute(near, axis, near_route)
    return near, far


def local(fluid_flux, margin_blocks, block_fluid, block_solid, diag_blocks, couple_blocks, couple_offset):
    owners = lax.axis_size("solid")
    groups = lax.axis_size("fluid")
    tiles = diag_blocks.shape[0]
    halo = tiles // 2
    total_blocks = block_fluid.shape[0]
    capacity = 5 * total_blocks // (2 * owners)
    chunk = capacity * 3 + ROWS

    sent = margin(block_fluid, block_solid, fluid_flux, margin_blocks, owners, tiles, chunk)
    received = lax.all_to_all(sent, "solid", split_axis=0, concat_axis=0, tiled=True)
    matrices = prepare(diag_blocks, couple_blocks)
    part = combine(received, owners, tiles)
    part1, part2, part3 = (
        lax.ppermute(part, "fluid", [(i, i ^ d) for i in range(groups)]) for d in (1, 2, 3)
    )
    whole = (tiles * ROWS, LANES)
    half = (halo * ROWS, LANES)
    pairs = pltpu.VMEM((tiles + halo, 2 * ROWS, LANES), F32)
    spread = pltpu.VMEM((tiles + halo, ROWS, LANES), F32)
    products = pltpu.VMEM((tiles, ROWS, LANES), F32)
    start, kept, near, far = call(
        functools.partial(first_send_kernel, tiles, halo),
        (whole, half, half, half),
        couple_offset,
        (part, part1, part3, part2, matrices),
        [pairs, spread, products],
        "first_send",
    )
    near, far = exchange(near, far, "solid")
    mapped, image = call(
        functools.partial(first_rest_kernel, tiles, halo),
        ((3, tiles, LANES), whole),
        couple_offset,
        (start, kept, matrices),
        [pairs, products, products],
        "first_rest",
        64,
    )
    vector1, inner, kept, leaving, near, far = call(
        functools.partial(second_send_kernel, tiles, halo),
        (whole, half, half, half, whole, whole),
        couple_offset,
        (image, far, near, matrices),
        [pairs, spread, products],
        "second_send",
    )
    near, far = exchange(near, far, "solid")
    outer, row = call(
        functools.partial(second_rest_kernel, tiles, halo),
        (half, (2 * ROWS, LANES)),
        couple_offset,
        (start, vector1, kept, matrices),
        [pairs],
        "second_rest",
        64,
    )
    vector2, moments = call(
        functools.partial(third_kernel, tiles, halo, owners - 1),
        (whole, (owners, LANES)),
        couple_offset,
        (vector1, inner, outer, leaving, row, far, near, matrices),
        [pairs],
        "third",
    )
    moments = moments.reshape(owners, 1, LANES)
    moments = lax.all_to_all(moments, "solid", split_axis=0, concat_axis=0, tiled=True)
    moments = moments.reshape(owners, LANES)
    nodal = pl.pallas_call(
        functools.partial(last_kernel, tiles),
        out_shape=jax.ShapeDtypeStruct((3, tiles, LANES), F32),
        in_specs=[VMEM] * 4,
        out_specs=VMEM,
        scratch_shapes=[pltpu.VMEM(whole, F32)],
        compiler_params=pltpu.CompilerParams(vmem_limit_bytes=4 << 20),
        name="last",
    )(moments, start, vector1, vector2)
    return mapped, nodal


def solution(mesh):
    in_specs = (
        P(None, ("fluid", "solid"), None),
        P(("fluid", "solid"), None, None),
        P(("fluid", "solid")),
        P(("fluid", "solid")),
        P("solid", None, None),
        P("solid", None, None),
        P("solid"),
    )
    out_specs = (P(None, "solid", None), P(None, "solid", None))
    return jax.shard_map(local, mesh=mesh, in_specs=in_specs, out_specs=out_specs, check_vma=False)
```

```python
import functools

import jax
import jax.numpy as jnp
from jax import lax
from jax.experimental import pallas as pl
from jax.experimental.pallas import tpu as pltpu
from jax.sharding import PartitionSpec as P

F32 = jnp.float32
BF16 = jnp.bfloat16
LANES = 128
ROWS = 4
SHIFT = 10.5
MOMENTS = 6
VMEM = pl.BlockSpec(memory_space=pltpu.VMEM)
SMEM = pl.BlockSpec(memory_space=pltpu.SMEM)
HBM = pl.BlockSpec(memory_space=pltpu.HBM)


def in_hbm(x):
    return pltpu.with_memory_space_constraint(x, pltpu.HBM)


def dot(a, b, contract=(1, 0)):
    return lax.dot_general(
        a, b, (((contract[0],), (contract[1],)), ((), ())), preferred_element_type=F32
    )


def split(x):
    high = x.astype(BF16).astype(F32)
    return high, x - high


def margin_kernel(owners, own_tiles, chunk, fluid_hbm, solid_hbm, flux_hbm, blocks_hbm, out, blocks, flux, left, right, fluid_ids, solid_ids, count, labels, sems):
    pieces = sems.shape[0] - 3
    size = blocks.shape[0] // pieces
    small = [
        pltpu.make_async_copy(source, target, sems.at[pieces + k])
        for k, (source, target) in enumerate(
            ((fluid_hbm, fluid_ids), (solid_hbm, solid_ids), (flux_hbm, flux))
        )
    ]

    def piece(k):
        part = pl.ds(k * size, size)
        return pltpu.make_async_copy(blocks_hbm.at[part], blocks.at[part], sems.at[k])

    for copy in small:
        copy.start()
    for k in range(pieces):
        piece(k).start()
    label_row = chunk - ROWS
    lane = lax.broadcasted_iota(jnp.int32, (1, LANES), 1)
    lane_first = jnp.where(lane < label_row, lane - lane % 3, -1)
    lane_field = lane % 3 * own_tiles
    out[...] = jnp.zeros_like(out)
    left[...] = jnp.zeros_like(left)
    right[...] = jnp.zeros_like(right)
    labels[...] = jnp.full_like(labels, -1.0)
    for owner in range(owners):
        count[owner] = 0
    for copy in small:
        copy.wait()
    for f in range(3):
        field = flux[f].astype(F32)
        left[pl.ds(f, flux.shape[1], stride=2 * ROWS), :] = field
        right[pl.ds(ROWS + f, flux.shape[1], stride=2 * ROWS), :] = field

    def place(block):
        solid = solid_ids[block]
        owner = lax.shift_right_logical(solid, own_tiles.bit_length() - 1)
        tile = solid & (own_tiles - 1)
        used = count[owner]
        count[owner] = used + 3
        label = (tile + lane_field).astype(F32)
        row = pl.ds(owner, 1)
        labels[row, :] = jnp.where(lane_first == used, label, labels[row, :])
        return owner * chunk + used

    def chosen(table, block):
        first = pl.multiple_of(fluid_ids[block] * (2 * ROWS), 2 * ROWS)
        return table[pl.ds(first, 2 * ROWS), :].astype(BF16)

    for k in range(pieces):
        piece(k).wait()
        for block in range(k * size, (k + 1) * size, 2):
            slots = place(block), place(block + 1)
            fields = jnp.concatenate([chosen(left, block), chosen(right, block + 1)], axis=1)
            terms = dot(fields, blocks[pl.ds(block, 2)].reshape(2 * LANES, LANES))
            for half, slot in enumerate(slots):
                for f in range(3):
                    row = half * ROWS + f
                    out[pl.ds(slot + f, 1), :] = terms[row : row + 1]
    for owner in range(owners):
        out[pl.ds(owner * chunk + label_row, 1), :] = labels[pl.ds(owner, 1), :]


def margin(fluid_ids, solid_ids, flux, blocks, owners, own_tiles, chunk):
    assert own_tiles & (own_tiles - 1) == 0
    pieces = 5
    assert blocks.shape[0] % (2 * pieces) == 0
    table = pltpu.VMEM((flux.shape[1] * 2 * ROWS, LANES), F32)
    return pl.pallas_call(
        functools.partial(margin_kernel, owners, own_tiles, chunk),
        out_shape=jax.ShapeDtypeStruct((owners * chunk, LANES), F32),
        in_specs=[HBM] * 4,
        out_specs=VMEM,
        scratch_shapes=[
            pltpu.VMEM(blocks.shape, BF16),
            pltpu.VMEM(flux.shape, BF16),
            table,
            table,
            pltpu.SMEM(fluid_ids.shape, jnp.int32),
            pltpu.SMEM(solid_ids.shape, jnp.int32),
            pltpu.SMEM((owners,), jnp.int32),
            pltpu.VMEM((owners, LANES), F32),
            pltpu.SemaphoreType.DMA((pieces + 3,)),
        ],
        compiler_params=pltpu.CompilerParams(vmem_limit_bytes=12 << 20),
        name="margin",
    )(*(in_hbm(x) for x in (fluid_ids, solid_ids, flux, blocks)))


def prepare_kernel(diag_hbm, couple_hbm, matrices, diag, couple, sems):
    pieces = sems.shape[1]
    size = diag.shape[0] // pieces

    def piece(k):
        part = pl.ds(k * size, size)
        return [
            pltpu.make_async_copy(source.at[part], target.at[part], sems.at[i, k])
            for i, (source, target) in enumerate(((diag_hbm, diag), (couple_hbm, couple)))
        ]

    for k in range(pieces):
        for copy in piece(k):
            copy.start()
    row = lax.broadcasted_iota(jnp.int32, (LANES, LANES), 0)
    column = lax.broadcasted_iota(jnp.int32, (LANES, LANES), 1)
    shift = jnp.where(row == column, SHIFT, 0.0).astype(F32)
    for k in range(pieces):
        for copy in piece(k):
            copy.wait()
        for t in range(k * size, (k + 1) * size):
            high, low = split(diag[t] - shift)
            matrices[t, 0:LANES, :] = high.astype(BF16)
            matrices[t, LANES : 2 * LANES, :] = low.astype(BF16)
            high, low = split(couple[t])
            matrices[t, 2 * LANES : 3 * LANES, :] = high.astype(BF16)
            matrices[t, 3 * LANES : 4 * LANES, :] = low.astype(BF16)
            matrices[t, 4 * LANES : 5 * LANES, :] = high.T.astype(BF16)
            matrices[t, 5 * LANES : 6 * LANES, :] = low.T.astype(BF16)


def prepare(diag, couple):
    tiles = diag.shape[0]
    return pl.pallas_call(
        prepare_kernel,
        out_shape=jax.ShapeDtypeStruct((tiles, 6 * LANES, LANES), BF16),
        in_specs=[HBM] * 2,
        out_specs=VMEM,
        scratch_shapes=[
            pltpu.VMEM(diag.shape, F32),
            pltpu.VMEM(couple.shape, F32),
            pltpu.SemaphoreType.DMA((2, 4)),
        ],
        compiler_params=pltpu.CompilerParams(vmem_limit_bytes=12 << 20),
        cost_estimate=pl.CostEstimate(flops=1 << 26, bytes_accessed=10 << 20, transcendentals=0),
        name="prepare",
    )(in_hbm(diag), in_hbm(couple))


def views(matrices):
    return tuple(matrices.at[:, 2 * k * LANES : 2 * (k + 1) * LANES, :] for k in range(3))


def combine_kernel(owners, received, out):
    chunk = received.shape[0] // owners
    row = lax.broadcasted_iota(jnp.int32, (out.shape[0], chunk), 0).astype(F32)
    total = jnp.zeros(out.shape, F32)
    for source in range(owners):
        values = received[source * chunk : (source + 1) * chunk, :]
        label = received[(source + 1) * chunk - ROWS : (source + 1) * chunk - ROWS + 1, 0:chunk]
        hits = (row == label).astype(F32).astype(BF16)
        high, low = split(values)
        total = total + dot(hits, high.astype(BF16)) + dot(hits, low.astype(BF16))
    out[...] = total


def combine(received, owners, own_tiles):
    return pl.pallas_call(
        functools.partial(combine_kernel, owners),
        out_shape=jax.ShapeDtypeStruct((own_tiles * 3, LANES), F32),
        in_specs=[VMEM],
        out_specs=VMEM,
        compiler_params=pltpu.CompilerParams(vmem_limit_bytes=16 << 20),
        name="combine",
    )(received)


def put_pairs(pairs, t, value):
    high, low = split(value)
    pairs[t, 0:ROWS, :] = high
    pairs[t, ROWS : 2 * ROWS, :] = low


def load_pairs(pairs, t):
    both = pairs[t].astype(BF16)
    return jnp.concatenate([both, both], axis=1)


def fold(product):
    return product[0:ROWS] + product[ROWS : 2 * ROWS]


def ahead(t, partner, pairs, turned):
    return fold(dot(load_pairs(pairs, partner), turned[t]))


def here(t, pairs, matrix):
    return fold(dot(load_pairs(pairs, t), matrix[t]))


def rows(t, count=1):
    return slice(t * ROWS, (t + count) * ROWS)


def select(flag, first, second):
    return jnp.where(flag > 0, first, second)


def add_transposed(tiles, arrived, pairs, spread, back, products, first, stop):
    for t in range(first, stop):
        products[t] = here(t, pairs, back)
    offsets = arrived()
    for t in range(first, stop):
        partner = t + offsets[t]
        spread[partner] = spread[partner] + products[t]


def first_send_kernel(tiles, halo, arrived, part0, part1, part3, part2, matrices, vector, kept, near, far, pairs, spread, products):
    own, back, turned = views(matrices)
    total = (part0[...] + part1[...]) + (part2[...] + part3[...])
    for f in range(3):
        vector[pl.ds(f, tiles, stride=ROWS), :] = total[f * tiles : (f + 1) * tiles]
    vector[pl.ds(3, tiles, stride=ROWS), :] = jnp.zeros((tiles, LANES), F32)
    for t in range(halo, tiles):
        put_pairs(pairs, t, vector[rows(t), :])
    spread[...] = jnp.zeros_like(spread)
    add_transposed(tiles, arrived, pairs, spread, back, products, halo, tiles)
    flag = lax.axis_index("solid") % 2
    for t in range(halo):
        rim = vector[rows(t), :]
        out = spread[tiles + t]
        near[rows(t), :] = select(flag, rim, out)
        far[rows(t), :] = select(flag, out, rim)
        kept[rows(t), :] = spread[halo + t]


def first_rest_kernel(tiles, halo, arrived, vector, kept, matrices, mapped, image, pairs, spread, products):
    own, back, turned = views(matrices)
    for f in range(3):
        mapped[f] = vector[pl.ds(f, tiles, stride=ROWS), :]
    for t in range(tiles):
        put_pairs(pairs, t, vector[rows(t), :])
    for t in range(tiles, tiles + halo):
        pairs[t] = jnp.zeros((2 * ROWS, LANES), F32)
    for t in range(halo):
        spread[t] = jnp.zeros((ROWS, LANES), F32)
        spread[halo + t] = kept[rows(t), :]
    offsets = arrived()
    add_transposed(tiles, lambda: offsets, pairs, spread, back, products, 0, halo)
    for t in range(tiles):
        value = here(t, pairs, own) + ahead(t, t + offsets[t], pairs, turned)
        image[rows(t), :] = spread[t] + value


def put_rim(tiles, halo, flag, near, far, pairs):
    for t in range(halo):
        put_pairs(pairs, tiles + t, select(flag, far[rows(t), :], near[rows(t), :]))
        pairs[tiles - halo + t] = jnp.zeros((2 * ROWS, LANES), F32)


def inner_part(t, offsets, pairs, spread, own, turned):
    return spread[t] + (here(t, pairs, own) + ahead(t, t + offsets[t], pairs, turned))


def second_far_kernel(tiles, halo, arrived, image, far, near, matrices, vector, far2, pairs, spread, products):
    own, back, turned = views(matrices)
    flag = lax.axis_index("solid") % 2
    size = halo * ROWS
    put_rim(tiles, halo, flag, near, far, pairs)
    offsets = arrived()
    vector[0:size, :] = image[0:size, :] + select(flag, near[...], far[...])
    for t in range(halo, tiles):
        partner = jnp.maximum(t + offsets[t], halo)
        vector[rows(t), :] = image[rows(t), :] + ahead(t, partner, pairs, turned)
    for t in range(tiles):
        put_pairs(pairs, t, vector[rows(t), :])
    spread[...] = jnp.zeros_like(spread)

    @pl.when(flag == 1)
    def _():
        add_transposed(tiles, lambda: offsets, pairs, spread, back, products, halo, tiles)
        for t in range(halo):
            far2[rows(t), :] = spread[tiles + t]
        far2[size : 2 * size, :] = jnp.zeros((size, LANES), F32)

    @pl.when(flag == 0)
    def _():
        add_transposed(tiles, lambda: offsets, pairs, spread, back, products, 0, halo)
        far2[0:size, :] = vector[0:size, :]
        for t in range(halo):
            far2[rows(halo + t), :] = inner_part(t, offsets, pairs, spread, own, turned)


def second_near_kernel(tiles, halo, arrived, vector, matrices, inner, kept, leaving, near2, pairs, spread, products):
    own, back, turned = views(matrices)
    flag = lax.axis_index("solid") % 2
    size = halo * ROWS
    for t in range(tiles):
        put_pairs(pairs, t, vector[rows(t), :])
    spread[...] = jnp.zeros_like(spread)
    offsets = arrived()
    add_transposed(tiles, lambda: offsets, pairs, spread, back, products, 0, tiles)
    for t in range(halo):
        inner[rows(t), :] = inner_part(t, offsets, pairs, spread, own, turned)
        kept[rows(t), :] = spread[halo + t]
        leaving[rows(t), :] = spread[tiles + t]
    near2[0:size, :] = select(flag, vector[0:size, :], leaving[...])
    near2[size : 2 * size, :] = inner[...]


def moment(a, b):
    folded = jnp.sum((a * b).reshape(-1, 2 * ROWS, LANES), axis=0)
    return jnp.sum(folded, axis=1, keepdims=True)


def placed(values, first):
    field = lax.broadcasted_iota(jnp.int32, (2 * ROWS, LANES), 0) % ROWS
    lane = lax.broadcasted_iota(jnp.int32, (2 * ROWS, LANES), 1)
    row = jnp.zeros((2 * ROWS, LANES), F32)
    for k, value in enumerate(values):
        row = row + jnp.where(lane == (first + k) * ROWS + field, value, 0.0)
    return row


def second_rest_kernel(tiles, halo, arrived, start, vector, kept, matrices, outer, row, pairs):
    own, back, turned = views(matrices)
    for t in range(halo, tiles):
        put_pairs(pairs, t, vector[rows(t), :])
    for t in range(tiles, tiles + halo):
        pairs[t] = jnp.zeros((2 * ROWS, LANES), F32)
    offsets = arrived()
    for t in range(halo, tiles):
        value = here(t, pairs, own) + ahead(t, t + offsets[t], pairs, turned)
        outer[rows(t - halo), :] = kept[rows(t - halo), :] + value
    v0, v1 = start[...], vector[...]
    row[...] = placed((moment(v0, v0), moment(v0, v1), moment(v1, v1)), 0)


def third_kernel(tiles, halo, last, arrived, vector1, inner, outer, leaving, row, far, near, matrices, vector2, out, pairs):
    own, back, turned = views(matrices)
    flag = lax.axis_index("solid") % 2
    put_rim(tiles, halo, flag, near, far, pairs)
    offsets = arrived()
    outside = [
        ahead(t, jnp.maximum(t + offsets[t], halo), pairs, turned) for t in range(halo, tiles)
    ]
    size = halo * ROWS
    vector2[0:size, :] = inner[...] + select(flag, near[0:size, :], far[0:size, :])
    for t in range(halo):
        put_pairs(pairs, t, vector2[rows(t), :])
    quadratic = jnp.zeros((ROWS, LANES), F32)
    for t in range(halo):
        quadratic = quadratic + vector2[rows(t), :] * here(t, pairs, own)
    for t in range(halo, tiles):
        value = outer[rows(t - halo), :] + outside[t - halo]
        vector2[rows(t), :] = value
        put_pairs(pairs, t, value)
    inside = jnp.where(lax.axis_index("solid") == last, 0.0, 1.0).astype(F32)
    for t in range(halo):
        other = rows(halo + t)
        rim = select(flag, far[other, :], near[other, :]) + leaving[rows(t), :]
        put_pairs(pairs, tiles + t, rim * inside)
    for t in range(halo, tiles):
        quadratic = quadratic + vector2[rows(t), :] * here(t, pairs, own)
    v1, v2 = vector1[...], vector2[...]
    total = row[...] + placed((moment(v1, v2), moment(v2, v2)), 3)
    coupled = jnp.zeros((ROWS, LANES), F32)
    for t in range(tiles):
        coupled = coupled + vector2[rows(t), :] * ahead(t, t + offsets[t], pairs, turned)
    quadratic = jnp.sum(quadratic + 2.0 * coupled, axis=1, keepdims=True)
    quadratic = jnp.concatenate([quadratic, jnp.zeros((ROWS, 1), F32)], axis=0)
    total = total + placed((quadratic,), 5)
    total = jnp.sum(total, axis=0, keepdims=True)
    out[...] = jnp.broadcast_to(total, out.shape)


def last_kernel(tiles, moments, start, vector1, vector2, nodal, mixed):
    total = jnp.sum(moments[...].reshape(-1, 2 * ROWS, LANES), axis=0)
    total = jnp.broadcast_to(jnp.sum(total, axis=0, keepdims=True), total.shape)
    g = [total if k == 0 else pltpu.roll(total, LANES - k * ROWS, 1) for k in range(MOMENTS)]
    h = [g[k + 1] + SHIFT * g[k] for k in range(MOMENTS - 1)]

    def form(table, c):
        n = len(c)
        result = None
        for i in range(n):
            for j in range(i, n):
                term = (c[i] * c[j]) * table[i + j]
                term = term if i == j else 2.0 * term
                result = term if result is None else result + term
        return result

    def apply(c):
        n = len(c)
        shifted = [SHIFT * c[0]]
        for i in range(1, n):
            shifted.append(c[i - 1] + SHIFT * c[i])
        return shifted + [c[n - 1]]

    one = jnp.ones_like(total)
    rr = g[0]
    alpha = rr / h[0]
    coefficients = [alpha]
    residual = [one - alpha * SHIFT, -alpha]
    new = form(g, residual)
    beta = new / rr
    direction = [residual[0] + beta, residual[1]]
    rr = new
    alpha = rr / form(h, direction)
    coefficients = [coefficients[0] + alpha * direction[0], alpha * direction[1]]
    image = apply(direction)
    residual = [residual[0] - alpha * image[0], residual[1] - alpha * image[1], -alpha * image[2]]
    new = form(g, residual)
    beta = new / rr
    direction = [residual[0] + beta * direction[0], residual[1] + beta * direction[1], residual[2]]
    rr = new
    alpha = rr / form(h, direction)
    coefficients = [
        coefficients[0] + alpha * direction[0],
        coefficients[1] + alpha * direction[1],
        alpha * direction[2],
    ]
    field = lax.broadcasted_iota(jnp.int32, (2 * ROWS, LANES), 0)
    lane = lax.broadcasted_iota(jnp.int32, (2 * ROWS, LANES), 1)
    result = jnp.zeros(start.shape, F32).reshape(-1, 2 * ROWS, LANES)
    for c, v in zip(coefficients, (start, vector1, vector2)):
        column = jnp.sum(jnp.where(lane == field % ROWS, c, 0.0), axis=1, keepdims=True)
        result = result + column[None] * v[...].reshape(-1, 2 * ROWS, LANES)
    mixed[...] = result.reshape(start.shape)
    for f in range(3):
        nodal[f] = mixed[pl.ds(f, tiles, stride=ROWS), :]


def with_offsets(kernel):
    def run(source, *refs):
        *refs, offsets, sem = refs
        copy = pltpu.make_async_copy(source, offsets, sem)
        copy.start()

        def arrived():
            copy.wait()
            return offsets

        kernel(arrived, *refs)

    return run


def call(kernel, shapes, offsets, vmem, scratch, name, work=0):
    estimate = pl.CostEstimate(flops=work << 20, bytes_accessed=work << 16, transcendentals=0)
    return pl.pallas_call(
        with_offsets(kernel),
        out_shape=tuple(jax.ShapeDtypeStruct(s, F32) for s in shapes),
        in_specs=[pl.BlockSpec(memory_space=pl.ANY)] + [VMEM] * len(vmem),
        out_specs=tuple(VMEM for _ in shapes),
        scratch_shapes=[
            *scratch,
            pltpu.SMEM(offsets.shape, jnp.int32),
            pltpu.SemaphoreType.DMA(()),
        ],
        compiler_params=pltpu.CompilerParams(vmem_limit_bytes=4 << 20),
        cost_estimate=estimate if work else None,
        name=name,
    )(offsets, *vmem)


def halo_routes(n):
    far_route = [(i, i + 1) for i in range(1, n - 1, 2)] + [(i + 1, i) for i in range(1, n - 1, 2)]
    near_route = [(i, i ^ 1) for i in range(n)]
    return near_route, far_route


def local(fluid_flux, margin_blocks, block_fluid, block_solid, diag_blocks, couple_blocks, couple_offset):
    owners = lax.axis_size("solid")
    groups = lax.axis_size("fluid")
    near_route, far_route = halo_routes(owners)
    tiles = diag_blocks.shape[0]
    halo = tiles // 2
    total_blocks = block_fluid.shape[0]
    capacity = 5 * total_blocks // (2 * owners)
    chunk = capacity * 3 + ROWS

    sent = margin(block_fluid, block_solid, fluid_flux, margin_blocks, owners, tiles, chunk)
    received = lax.all_to_all(sent, "solid", split_axis=0, concat_axis=0, tiled=True)
    matrices = prepare(diag_blocks, couple_blocks)
    part = combine(received, owners, tiles)
    part1, part2, part3 = (
        lax.ppermute(part, "fluid", [(i, i ^ d) for i in range(groups)]) for d in (1, 2, 3)
    )
    whole = (tiles * ROWS, LANES)
    half = (halo * ROWS, LANES)
    pairs = pltpu.VMEM((tiles + halo, 2 * ROWS, LANES), F32)
    spread = pltpu.VMEM((tiles + halo, ROWS, LANES), F32)
    products = pltpu.VMEM((tiles, ROWS, LANES), F32)
    start, kept, near, far = call(
        functools.partial(first_send_kernel, tiles, halo),
        (whole, half, half, half),
        couple_offset,
        (part, part1, part3, part2, matrices),
        [pairs, spread, products],
        "first_send",
    )
    far = lax.ppermute(far, "solid", far_route)
    near = lax.ppermute(near, "solid", near_route)
    mapped, image = call(
        functools.partial(first_rest_kernel, tiles, halo),
        ((3, tiles, LANES), whole),
        couple_offset,
        (start, kept, matrices),
        [pairs, products, products],
        "first_rest",
        64,
    )
    vector1, far = call(
        functools.partial(second_far_kernel, tiles, halo),
        (whole, whole),
        couple_offset,
        (image, far, near, matrices),
        [pairs, spread, products],
        "second_far",
    )
    far = lax.ppermute(far, "solid", far_route)
    inner, kept, leaving, near = call(
        functools.partial(second_near_kernel, tiles, halo),
        (half, half, half, whole),
        couple_offset,
        (vector1, matrices),
        [pairs, spread, products],
        "second_near",
        64,
    )
    near = lax.ppermute(near, "solid", near_route)
    outer, row = call(
        functools.partial(second_rest_kernel, tiles, halo),
        (half, (2 * ROWS, LANES)),
        couple_offset,
        (start, vector1, kept, matrices),
        [pairs],
        "second_rest",
        64,
    )
    vector2, moments = call(
        functools.partial(third_kernel, tiles, halo, owners - 1),
        (whole, (owners, LANES)),
        couple_offset,
        (vector1, inner, outer, leaving, row, far, near, matrices),
        [pairs],
        "third",
    )
    moments = moments.reshape(owners, 1, LANES)
    moments = lax.all_to_all(moments, "solid", split_axis=0, concat_axis=0, tiled=True)
    moments = moments.reshape(owners, LANES)
    nodal = pl.pallas_call(
        functools.partial(last_kernel, tiles),
        out_shape=jax.ShapeDtypeStruct((3, tiles, LANES), F32),
        in_specs=[VMEM] * 4,
        out_specs=VMEM,
        scratch_shapes=[pltpu.VMEM(whole, F32)],
        compiler_params=pltpu.CompilerParams(vmem_limit_bytes=4 << 20),
        name="last",
    )(moments, start, vector1, vector2)
    return mapped, nodal


def solution(mesh):
    in_specs = (
        P(None, ("fluid", "solid"), None),
        P(("fluid", "solid"), None, None),
        P(("fluid", "solid")),
        P(("fluid", "solid")),
        P("solid", None, None),
        P("solid", None, None),
        P("solid"),
    )
    out_specs = (P(None, "solid", None), P(None, "solid", None))
    return jax.shard_map(local, mesh=mesh, in_specs=in_specs, out_specs=out_specs, check_vma=False)
```

```python
import functools

import jax
import jax.numpy as jnp
from jax import lax
from jax.experimental import pallas as pl
from jax.experimental.pallas import tpu as pltpu
from jax.sharding import PartitionSpec as P

F32 = jnp.float32
BF16 = jnp.bfloat16
LANES = 128
ROWS = 4
SHIFT = 10.5
MOMENTS = 6
VMEM = pl.BlockSpec(memory_space=pltpu.VMEM)
SMEM = pl.BlockSpec(memory_space=pltpu.SMEM)
HBM = pl.BlockSpec(memory_space=pltpu.HBM)


def in_hbm(x):
    return pltpu.with_memory_space_constraint(x, pltpu.HBM)


def dot(a, b, contract=(1, 0)):
    return lax.dot_general(
        a, b, (((contract[0],), (contract[1],)), ((), ())), preferred_element_type=F32
    )


def split(x):
    high = x.astype(BF16).astype(F32)
    return high, x - high


def margin_kernel(owners, own_tiles, chunk, fluid_hbm, solid_hbm, flux_hbm, blocks_hbm, out, blocks, flux, left, right, fluid_ids, solid_ids, count, labels, sems):
    pieces = sems.shape[0] - 3
    size = blocks.shape[0] // pieces
    small = [
        pltpu.make_async_copy(source, target, sems.at[pieces + k])
        for k, (source, target) in enumerate(
            ((fluid_hbm, fluid_ids), (solid_hbm, solid_ids), (flux_hbm, flux))
        )
    ]

    def piece(k):
        part = pl.ds(k * size, size)
        return pltpu.make_async_copy(blocks_hbm.at[part], blocks.at[part], sems.at[k])

    for copy in small:
        copy.start()
    for k in range(pieces):
        piece(k).start()
    label_row = chunk - ROWS
    lane = lax.broadcasted_iota(jnp.int32, (1, LANES), 1)
    lane_first = jnp.where(lane < label_row, lane - lane % 3, -1)
    lane_field = lane % 3 * own_tiles
    out[...] = jnp.zeros_like(out)
    left[...] = jnp.zeros_like(left)
    right[...] = jnp.zeros_like(right)
    labels[...] = jnp.full_like(labels, -1.0)
    for owner in range(owners):
        count[owner] = 0
    for copy in small:
        copy.wait()
    for f in range(3):
        field = flux[f].astype(F32)
        left[pl.ds(f, flux.shape[1], stride=2 * ROWS), :] = field
        right[pl.ds(ROWS + f, flux.shape[1], stride=2 * ROWS), :] = field

    def place(block):
        solid = solid_ids[block]
        owner = lax.shift_right_logical(solid, own_tiles.bit_length() - 1)
        tile = solid & (own_tiles - 1)
        used = count[owner]
        count[owner] = used + 3
        label = (tile + lane_field).astype(F32)
        row = pl.ds(owner, 1)
        labels[row, :] = jnp.where(lane_first == used, label, labels[row, :])
        return owner * chunk + used

    def chosen(table, block):
        first = pl.multiple_of(fluid_ids[block] * (2 * ROWS), 2 * ROWS)
        return table[pl.ds(first, 2 * ROWS), :].astype(BF16)

    for k in range(pieces):
        piece(k).wait()
        for block in range(k * size, (k + 1) * size, 2):
            slots = place(block), place(block + 1)
            fields = jnp.concatenate([chosen(left, block), chosen(right, block + 1)], axis=1)
            terms = dot(fields, blocks[pl.ds(block, 2)].reshape(2 * LANES, LANES))
            for half, slot in enumerate(slots):
                for f in range(3):
                    row = half * ROWS + f
                    out[pl.ds(slot + f, 1), :] = terms[row : row + 1]
    for owner in range(owners):
        out[pl.ds(owner * chunk + label_row, 1), :] = labels[pl.ds(owner, 1), :]


def margin(fluid_ids, solid_ids, flux, blocks, owners, own_tiles, chunk):
    assert own_tiles & (own_tiles - 1) == 0
    pieces = 8
    assert blocks.shape[0] % (2 * pieces) == 0
    table = pltpu.VMEM((flux.shape[1] * 2 * ROWS, LANES), F32)
    return pl.pallas_call(
        functools.partial(margin_kernel, owners, own_tiles, chunk),
        out_shape=jax.ShapeDtypeStruct((owners * chunk, LANES), F32),
        in_specs=[HBM] * 4,
        out_specs=VMEM,
        scratch_shapes=[
            pltpu.VMEM(blocks.shape, BF16),
            pltpu.VMEM(flux.shape, BF16),
            table,
            table,
            pltpu.SMEM(fluid_ids.shape, jnp.int32),
            pltpu.SMEM(solid_ids.shape, jnp.int32),
            pltpu.SMEM((owners,), jnp.int32),
            pltpu.VMEM((owners, LANES), F32),
            pltpu.SemaphoreType.DMA((pieces + 3,)),
        ],
        compiler_params=pltpu.CompilerParams(vmem_limit_bytes=12 << 20),
        name="margin",
    )(*(in_hbm(x) for x in (fluid_ids, solid_ids, flux, blocks)))


def prepare_kernel(diag_hbm, couple_hbm, matrices, diag, couple, sems):
    pieces = sems.shape[1]
    size = diag.shape[0] // pieces

    def piece(k):
        part = pl.ds(k * size, size)
        return [
            pltpu.make_async_copy(source.at[part], target.at[part], sems.at[i, k])
            for i, (source, target) in enumerate(((diag_hbm, diag), (couple_hbm, couple)))
        ]

    for k in range(pieces):
        for copy in piece(k):
            copy.start()
    row = lax.broadcasted_iota(jnp.int32, (LANES, LANES), 0)
    column = lax.broadcasted_iota(jnp.int32, (LANES, LANES), 1)
    shift = jnp.where(row == column, SHIFT, 0.0).astype(F32)
    for k in range(pieces):
        for copy in piece(k):
            copy.wait()
        for t in range(k * size, (k + 1) * size):
            high, low = split(diag[t] - shift)
            matrices[t, 0:LANES, :] = high.astype(BF16)
            matrices[t, LANES : 2 * LANES, :] = low.astype(BF16)
            high, low = split(couple[t])
            matrices[t, 2 * LANES : 3 * LANES, :] = high.astype(BF16)
            matrices[t, 3 * LANES : 4 * LANES, :] = low.astype(BF16)
            matrices[t, 4 * LANES : 5 * LANES, :] = high.T.astype(BF16)
            matrices[t, 5 * LANES : 6 * LANES, :] = low.T.astype(BF16)


def prepare(diag, couple):
    tiles = diag.shape[0]
    return pl.pallas_call(
        prepare_kernel,
        out_shape=jax.ShapeDtypeStruct((tiles, 6 * LANES, LANES), BF16),
        in_specs=[HBM] * 2,
        out_specs=VMEM,
        scratch_shapes=[
            pltpu.VMEM(diag.shape, F32),
            pltpu.VMEM(couple.shape, F32),
            pltpu.SemaphoreType.DMA((2, 4)),
        ],
        compiler_params=pltpu.CompilerParams(vmem_limit_bytes=12 << 20),
        cost_estimate=pl.CostEstimate(flops=1 << 26, bytes_accessed=10 << 20, transcendentals=0),
        name="prepare",
    )(in_hbm(diag), in_hbm(couple))


def views(matrices):
    return tuple(matrices.at[:, 2 * k * LANES : 2 * (k + 1) * LANES, :] for k in range(3))


def combine_kernel(owners, received, out):
    chunk = received.shape[0] // owners
    row = lax.broadcasted_iota(jnp.int32, (out.shape[0], chunk), 0).astype(F32)
    total = jnp.zeros(out.shape, F32)
    for source in range(owners):
        values = received[source * chunk : (source + 1) * chunk, :]
        label = received[(source + 1) * chunk - ROWS : (source + 1) * chunk - ROWS + 1, 0:chunk]
        hits = (row == label).astype(F32).astype(BF16)
        high, low = split(values)
        total = total + dot(hits, high.astype(BF16)) + dot(hits, low.astype(BF16))
    out[...] = total


def combine(received, owners, own_tiles):
    return pl.pallas_call(
        functools.partial(combine_kernel, owners),
        out_shape=jax.ShapeDtypeStruct((own_tiles * 3, LANES), F32),
        in_specs=[VMEM],
        out_specs=VMEM,
        compiler_params=pltpu.CompilerParams(vmem_limit_bytes=16 << 20),
        name="combine",
    )(received)


def put_pairs(pairs, t, value):
    high, low = split(value)
    pairs[t, 0:ROWS, :] = high
    pairs[t, ROWS : 2 * ROWS, :] = low


def load_pairs(pairs, t):
    both = pairs[t].astype(BF16)
    return jnp.concatenate([both, both], axis=1)


def fold(product):
    return product[0:ROWS] + product[ROWS : 2 * ROWS]


def ahead(t, partner, pairs, turned):
    return fold(dot(load_pairs(pairs, partner), turned[t]))


def here(t, pairs, matrix):
    return fold(dot(load_pairs(pairs, t), matrix[t]))


def rows(t, count=1):
    return slice(t * ROWS, (t + count) * ROWS)


def select(flag, first, second):
    return jnp.where(flag > 0, first, second)


def add_transposed(tiles, arrived, pairs, spread, back, products, first, stop):
    for t in range(first, stop):
        products[t] = here(t, pairs, back)
    offsets = arrived()
    for t in range(first, stop):
        partner = t + offsets[t]
        spread[partner] = spread[partner] + products[t]


def first_send_kernel(tiles, halo, arrived, part0, part1, part3, part2, matrices, vector, kept, near, far, pairs, spread, products):
    own, back, turned = views(matrices)
    total = (part0[...] + part1[...]) + (part2[...] + part3[...])
    for f in range(3):
        vector[pl.ds(f, tiles, stride=ROWS), :] = total[f * tiles : (f + 1) * tiles]
    vector[pl.ds(3, tiles, stride=ROWS), :] = jnp.zeros((tiles, LANES), F32)
    for t in range(halo, tiles):
        put_pairs(pairs, t, vector[rows(t), :])
    spread[...] = jnp.zeros_like(spread)
    add_transposed(tiles, arrived, pairs, spread, back, products, halo, tiles)
    flag = lax.axis_index("solid") % 2
    for t in range(halo):
        rim = vector[rows(t), :]
        out = spread[tiles + t]
        near[rows(t), :] = select(flag, rim, out)
        far[rows(t), :] = select(flag, out, rim)
        kept[rows(t), :] = spread[halo + t]


def first_rest_kernel(tiles, halo, arrived, vector, kept, matrices, mapped, image, pairs, spread, products):
    own, back, turned = views(matrices)
    for f in range(3):
        mapped[f] = vector[pl.ds(f, tiles, stride=ROWS), :]
    for t in range(tiles):
        put_pairs(pairs, t, vector[rows(t), :])
    for t in range(tiles, tiles + halo):
        pairs[t] = jnp.zeros((2 * ROWS, LANES), F32)
    for t in range(halo):
        spread[t] = jnp.zeros((ROWS, LANES), F32)
        spread[halo + t] = kept[rows(t), :]
    offsets = arrived()
    add_transposed(tiles, lambda: offsets, pairs, spread, back, products, 0, halo)
    for t in range(tiles):
        value = here(t, pairs, own) + ahead(t, t + offsets[t], pairs, turned)
        image[rows(t), :] = spread[t] + value


def put_rim(tiles, halo, flag, near, far, pairs):
    for t in range(halo):
        put_pairs(pairs, tiles + t, select(flag, far[rows(t), :], near[rows(t), :]))
        pairs[tiles - halo + t] = jnp.zeros((2 * ROWS, LANES), F32)


def second_send_kernel(tiles, halo, arrived, image, far, near, matrices, vector, inner, kept, leaving, near2, far2, pairs, spread, products):
    own, back, turned = views(matrices)
    flag = lax.axis_index("solid") % 2
    put_rim(tiles, halo, flag, near, far, pairs)
    offsets = arrived()
    for t in range(halo):
        vector[rows(t), :] = image[rows(t), :] + select(flag, near[rows(t), :], far[rows(t), :])
    for t in range(halo, tiles):
        partner = jnp.maximum(t + offsets[t], halo)
        vector[rows(t), :] = image[rows(t), :] + ahead(t, partner, pairs, turned)
    for t in range(tiles):
        put_pairs(pairs, t, vector[rows(t), :])
    spread[...] = jnp.zeros_like(spread)
    add_transposed(tiles, lambda: offsets, pairs, spread, back, products, 0, tiles)
    size = halo * ROWS
    for t in range(halo):
        inner[rows(t), :] = spread[t] + (here(t, pairs, own) + ahead(t, t + offsets[t], pairs, turned))
        kept[rows(t), :] = spread[halo + t]
        leaving[rows(t), :] = spread[tiles + t]
    near2[0:size, :] = select(flag, vector[0:size, :], leaving[...])
    far2[0:size, :] = select(flag, leaving[...], vector[0:size, :])
    near2[size : 2 * size, :] = inner[...]
    far2[size : 2 * size, :] = inner[...]


def moment(a, b):
    folded = jnp.sum((a * b).reshape(-1, 2 * ROWS, LANES), axis=0)
    return jnp.sum(folded, axis=1, keepdims=True)


def placed(values, first):
    field = lax.broadcasted_iota(jnp.int32, (2 * ROWS, LANES), 0) % ROWS
    lane = lax.broadcasted_iota(jnp.int32, (2 * ROWS, LANES), 1)
    row = jnp.zeros((2 * ROWS, LANES), F32)
    for k, value in enumerate(values):
        row = row + jnp.where(lane == (first + k) * ROWS + field, value, 0.0)
    return row


def second_rest_kernel(tiles, halo, arrived, start, vector, kept, matrices, outer, row, pairs):
    own, back, turned = views(matrices)
    for t in range(halo, tiles):
        put_pairs(pairs, t, vector[rows(t), :])
    for t in range(tiles, tiles + halo):
        pairs[t] = jnp.zeros((2 * ROWS, LANES), F32)
    offsets = arrived()
    for t in range(halo, tiles):
        value = here(t, pairs, own) + ahead(t, t + offsets[t], pairs, turned)
        outer[rows(t - halo), :] = kept[rows(t - halo), :] + value
    v0, v1 = start[...], vector[...]
    row[...] = placed((moment(v0, v0), moment(v0, v1), moment(v1, v1)), 0)


def third_kernel(tiles, halo, last, arrived, vector1, inner, outer, leaving, row, far, near, matrices, vector2, out, pairs):
    own, back, turned = views(matrices)
    flag = lax.axis_index("solid") % 2
    put_rim(tiles, halo, flag, near, far, pairs)
    offsets = arrived()
    outside = [
        ahead(t, jnp.maximum(t + offsets[t], halo), pairs, turned) for t in range(halo, tiles)
    ]
    size = halo * ROWS
    vector2[0:size, :] = inner[...] + select(flag, near[0:size, :], far[0:size, :])
    for t in range(halo):
        put_pairs(pairs, t, vector2[rows(t), :])
    quadratic = jnp.zeros((ROWS, LANES), F32)
    for t in range(halo):
        quadratic = quadratic + vector2[rows(t), :] * here(t, pairs, own)
    for t in range(halo, tiles):
        value = outer[rows(t - halo), :] + outside[t - halo]
        vector2[rows(t), :] = value
        put_pairs(pairs, t, value)
    inside = jnp.where(lax.axis_index("solid") == last, 0.0, 1.0).astype(F32)
    for t in range(halo):
        other = rows(halo + t)
        rim = select(flag, far[other, :], near[other, :]) + leaving[rows(t), :]
        put_pairs(pairs, tiles + t, rim * inside)
    for t in range(halo, tiles):
        quadratic = quadratic + vector2[rows(t), :] * here(t, pairs, own)
    v1, v2 = vector1[...], vector2[...]
    total = row[...] + placed((moment(v1, v2), moment(v2, v2)), 3)
    coupled = jnp.zeros((ROWS, LANES), F32)
    for t in range(tiles):
        coupled = coupled + vector2[rows(t), :] * ahead(t, t + offsets[t], pairs, turned)
    quadratic = jnp.sum(quadratic + 2.0 * coupled, axis=1, keepdims=True)
    quadratic = jnp.concatenate([quadratic, jnp.zeros((ROWS, 1), F32)], axis=0)
    total = total + placed((quadratic,), 5)
    total = jnp.sum(total, axis=0, keepdims=True)
    out[...] = jnp.broadcast_to(total, out.shape)


def last_kernel(tiles, moments, start, vector1, vector2, nodal, mixed):
    total = jnp.sum(moments[...].reshape(-1, 2 * ROWS, LANES), axis=0)
    total = jnp.broadcast_to(jnp.sum(total, axis=0, keepdims=True), total.shape)
    g = [total if k == 0 else pltpu.roll(total, LANES - k * ROWS, 1) for k in range(MOMENTS)]
    h = [g[k + 1] + SHIFT * g[k] for k in range(MOMENTS - 1)]

    def form(table, c):
        n = len(c)
        result = None
        for i in range(n):
            for j in range(i, n):
                term = (c[i] * c[j]) * table[i + j]
                term = term if i == j else 2.0 * term
                result = term if result is None else result + term
        return result

    def apply(c):
        n = len(c)
        shifted = [SHIFT * c[0]]
        for i in range(1, n):
            shifted.append(c[i - 1] + SHIFT * c[i])
        return shifted + [c[n - 1]]

    one = jnp.ones_like(total)
    rr = g[0]
    alpha = rr / h[0]
    coefficients = [alpha]
    residual = [one - alpha * SHIFT, -alpha]
    new = form(g, residual)
    beta = new / rr
    direction = [residual[0] + beta, residual[1]]
    rr = new
    alpha = rr / form(h, direction)
    coefficients = [coefficients[0] + alpha * direction[0], alpha * direction[1]]
    image = apply(direction)
    residual = [residual[0] - alpha * image[0], residual[1] - alpha * image[1], -alpha * image[2]]
    new = form(g, residual)
    beta = new / rr
    direction = [residual[0] + beta * direction[0], residual[1] + beta * direction[1], residual[2]]
    rr = new
    alpha = rr / form(h, direction)
    coefficients = [
        coefficients[0] + alpha * direction[0],
        coefficients[1] + alpha * direction[1],
        alpha * direction[2],
    ]
    field = lax.broadcasted_iota(jnp.int32, (2 * ROWS, LANES), 0)
    lane = lax.broadcasted_iota(jnp.int32, (2 * ROWS, LANES), 1)
    result = jnp.zeros(start.shape, F32).reshape(-1, 2 * ROWS, LANES)
    for c, v in zip(coefficients, (start, vector1, vector2)):
        column = jnp.sum(jnp.where(lane == field % ROWS, c, 0.0), axis=1, keepdims=True)
        result = result + column[None] * v[...].reshape(-1, 2 * ROWS, LANES)
    mixed[...] = result.reshape(start.shape)
    for f in range(3):
        nodal[f] = mixed[pl.ds(f, tiles, stride=ROWS), :]


def with_offsets(kernel):
    def run(source, *refs):
        *refs, offsets, sem = refs
        copy = pltpu.make_async_copy(source, offsets, sem)
        copy.start()

        def arrived():
            copy.wait()
            return offsets

        kernel(arrived, *refs)

    return run


def call(kernel, shapes, offsets, vmem, scratch, name, work=0):
    estimate = pl.CostEstimate(flops=work << 20, bytes_accessed=work << 16, transcendentals=0)
    return pl.pallas_call(
        with_offsets(kernel),
        out_shape=tuple(jax.ShapeDtypeStruct(s, F32) for s in shapes),
        in_specs=[pl.BlockSpec(memory_space=pl.ANY)] + [VMEM] * len(vmem),
        out_specs=tuple(VMEM for _ in shapes),
        scratch_shapes=[
            *scratch,
            pltpu.SMEM(offsets.shape, jnp.int32),
            pltpu.SemaphoreType.DMA(()),
        ],
        compiler_params=pltpu.CompilerParams(vmem_limit_bytes=4 << 20),
        cost_estimate=estimate if work else None,
        name=name,
    )(offsets, *vmem)


def exchange(near, far, axis):
    n = lax.axis_size(axis)
    far_route = [(i, i + 1) for i in range(1, n - 1, 2)] + [(i + 1, i) for i in range(1, n - 1, 2)]
    near_route = [(i, i ^ 1) for i in range(n)]
    far = lax.ppermute(far, axis, far_route)
    near = lax.ppermute(near, axis, near_route)
    return near, far


def local(fluid_flux, margin_blocks, block_fluid, block_solid, diag_blocks, couple_blocks, couple_offset):
    owners = lax.axis_size("solid")
    groups = lax.axis_size("fluid")
    tiles = diag_blocks.shape[0]
    halo = tiles // 2
    total_blocks = block_fluid.shape[0]
    capacity = 5 * total_blocks // (2 * owners)
    chunk = capacity * 3 + ROWS

    sent = margin(block_fluid, block_solid, fluid_flux, margin_blocks, owners, tiles, chunk)
    received = lax.all_to_all(sent, "solid", split_axis=0, concat_axis=0, tiled=True)
    matrices = prepare(diag_blocks, couple_blocks)
    part = combine(received, owners, tiles)
    part1, part2, part3 = (
        lax.ppermute(part, "fluid", [(i, i ^ d) for i in range(groups)]) for d in (1, 2, 3)
    )
    whole = (tiles * ROWS, LANES)
    half = (halo * ROWS, LANES)
    pairs = pltpu.VMEM((tiles + halo, 2 * ROWS, LANES), F32)
    spread = pltpu.VMEM((tiles + halo, ROWS, LANES), F32)
    products = pltpu.VMEM((tiles, ROWS, LANES), F32)
    start, kept, near, far = call(
        functools.partial(first_send_kernel, tiles, halo),
        (whole, half, half, half),
        couple_offset,
        (part, part1, part3, part2, matrices),
        [pairs, spread, products],
        "first_send",
    )
    near, far = exchange(near, far, "solid")
    mapped, image = call(
        functools.partial(first_rest_kernel, tiles, halo),
        ((3, tiles, LANES), whole),
        couple_offset,
        (start, kept, matrices),
        [pairs, products, products],
        "first_rest",
        64,
    )
    vector1, inner, kept, leaving, near, far = call(
        functools.partial(second_send_kernel, tiles, halo),
        (whole, half, half, half, whole, whole),
        couple_offset,
        (image, far, near, matrices),
        [pairs, spread, products],
        "second_send",
    )
    near, far = exchange(near, far, "solid")
    outer, row = call(
        functools.partial(second_rest_kernel, tiles, halo),
        (half, (2 * ROWS, LANES)),
        couple_offset,
        (start, vector1, kept, matrices),
        [pairs],
        "second_rest",
        64,
    )
    vector2, moments = call(
        functools.partial(third_kernel, tiles, halo, owners - 1),
        (whole, (owners, LANES)),
        couple_offset,
        (vector1, inner, outer, leaving, row, far, near, matrices),
        [pairs],
        "third",
    )
    moments = moments.reshape(owners, 1, LANES)
    moments = lax.all_to_all(moments, "solid", split_axis=0, concat_axis=0, tiled=True)
    moments = moments.reshape(owners, LANES)
    nodal = pl.pallas_call(
        functools.partial(last_kernel, tiles),
        out_shape=jax.ShapeDtypeStruct((3, tiles, LANES), F32),
        in_specs=[VMEM] * 4,
        out_specs=VMEM,
        scratch_shapes=[pltpu.VMEM(whole, F32)],
        compiler_params=pltpu.CompilerParams(vmem_limit_bytes=4 << 20),
        name="last",
    )(moments, start, vector1, vector2)
    return mapped, nodal


def solution(mesh):
    in_specs = (
        P(None, ("fluid", "solid"), None),
        P(("fluid", "solid"), None, None),
        P(("fluid", "solid")),
        P(("fluid", "solid")),
        P("solid", None, None),
        P("solid", None, None),
        P("solid"),
    )
    out_specs = (P(None, "solid", None), P(None, "solid", None))
    return jax.shard_map(local, mesh=mesh, in_specs=in_specs, out_specs=out_specs, check_vma=False)
```
